32 devices in a mesh: rep: 8 (over y, x, core), shard: 4 (over z).
Axes of the slice: x: 2, y: 2, z: 4, core: 2. Of those that a mesh axis runs over, the one named last changes fastest.
Arguments:
- tokens: bfloat16 [8192, 512], P(('rep', 'shard')), may hold values from -6 to 6
- cotangent: bfloat16 [8192, 512], P(('rep', 'shard')), may hold values from -6 to 6
- block_fill: int32 [64], P(('rep', 'shard')), may hold values from 0 to 128, as said below
- block_start: int32 [64], P(('rep', 'shard')), may hold values from 0 to 1, as said below
- in_weight: float32 [512, 2320], P('shard'), may hold values from -0.25 to 0.25
- out_weight: float32 [1024, 512], P('shard'), may hold values from -0.1875 to 0.1875
- in_moment: float32 [512, 2320], P('shard'), may hold values from -1.5 to 1.5
- out_moment: float32 [1024, 512], P('shard'), may hold values from -4 to 4
- norm_gain: float32 [512], replicated, may hold values from 0.5 to 1.5
- gate_gain: float32 [1024], replicated, may hold values from 0.5 to 1.5
- conv_params: float32 [5, 1280], replicated, may hold values from -0.5 to 0.5
- head_params: float32 [3, 16], replicated, may hold values from -6.3 to 1.5
- adam_norm: float32 [2, 512], replicated, may hold values from -0.2 to 0.2, as said below
- adam_gate: float32 [2, 1024], replicated, may hold values from -0.2 to 0.2, as said below
- adam_conv: float32 [2, 5, 1280], replicated, may hold values from -0.2 to 0.2, as said below
- adam_head: float32 [2, 3, 16], replicated, may hold values from -0.2 to 0.2, as said below
Outputs:
- activations: bfloat16 [8192, 512], P(('rep', 'shard'))
- input_grad: float32 [8192, 512], P(('rep', 'shard'))
- grad_in_weight: float32 [512, 2320], P('shard')
- grad_out_weight: float32 [1024, 512], P('shard')
- grad_norm_gain: float32 [512], replicated
- grad_gate_gain: float32 [1024], replicated
- grad_conv: float32 [5, 1280], replicated
- grad_head: float32 [3, 16], replicated
- new_in_weight: float32 [512, 2320], P('shard')
- new_out_weight: float32 [1024, 512], P('shard')
- new_in_moment: float32 [512, 2320], P('shard')
- new_out_moment: float32 [1024, 512], P('shard')
- new_norm_gain: float32 [512], replicated
- new_gate_gain: float32 [1024], replicated
- new_conv_params: float32 [5, 1280], replicated
- new_head_params: float32 [3, 16], replicated
- new_adam_norm: float32 [2, 512], replicated
- new_adam_gate: float32 [2, 1024], replicated
- new_adam_conv: float32 [2, 5, 1280], replicated
- new_adam_head: float32 [2, 3, 16], replicated
The draws below stay inside these ranges and needn't reach their ends.
Inputs may be any that keep to these rules, and one draw needn't show every extreme that they name: Each device holds 2 blocks of 128 slots, in order; a block's first block_fill slots hold tokens of one sequence and the rest are padding. A sequence fills every block but its last. Some device holds a sequence of 256 tokens, and some device has an empty block. `block_start`: 1 on every device's first block, on every block that follows a partly filled or empty one, and on empty blocks; 0 only where the block before is full and the sequence goes on. `adam_norm`: second moments are positive. `adam_gate`: second moments are positive. `adam_conv`: second moments are positive. `adam_head`: second moments are positive.
All inputs are finite; a program needn't handle non-finite values.
Results may differ from the reference program's by a relative error of at most 0.0085.
The reference program's roundings to bfloat16 on the way count: a program that leaves them out, or rounds other values in their place, can miss the bound.
Values may be sent and summed in bfloat16 or wider, within the bound.
A program may use at most 128 MiB of HBM per device.

```python
import math
import jax
import jax.numpy as jnp
from jax import lax

D = 512
H = 16
K = 4
BLOCK_LEN = 128
BLOCKS_DEV = 2
NS_STEPS = 5
ADAM_STEP = 3
E = 1024
CONV_CH = 1280
IN_COLS = 2320
TOK_DEV = 256
TOKENS = 8192
N_BLOCKS = 64


def deal_blocks(key):
    devices = N_BLOCKS // BLOCKS_DEV
    subkeys = jax.random.split(key, 4)
    pattern = jax.random.randint(subkeys[0], (devices,), 0, 3)
    pattern = pattern.at[0].set(0).at[1].set(2)
    first_len = jax.random.randint(subkeys[1], (devices,), 1, BLOCK_LEN + 1)
    second_len = jax.random.randint(subkeys[2], (devices,), 1, BLOCK_LEN + 1)
    tail_len = jax.random.randint(subkeys[3], (devices,), 1, BLOCK_LEN + 1).at[0].set(BLOCK_LEN)
    fill_first = jnp.where(pattern == 0, BLOCK_LEN, first_len)
    fill_second = jnp.where(pattern == 0, tail_len, jnp.where(pattern == 1, second_len, 0))
    start_second = jnp.where(pattern == 0, 0, 1)
    fills = jnp.stack([fill_first, fill_second], 1).reshape(-1).astype(jnp.int32)
    starts = jnp.stack([jnp.ones_like(start_second), start_second], 1).reshape(-1).astype(jnp.int32)
    return (fills, starts)


def draw_block_fill(key, part):
    return deal_blocks(jax.random.fold_in(key, 11))[0]


def draw_block_start(key, part):
    return deal_blocks(jax.random.fold_in(key, 11))[1]


def draw_head_params(key, part):
    subkeys = jax.random.split(key, 3)
    bias_row = jax.random.uniform(subkeys[0], (H,), jnp.float32, -1.0, 1.0)
    rate_row = jax.random.uniform(subkeys[1], (H,), jnp.float32, math.log(0.002), math.log(0.1))
    skip_row = jax.random.uniform(subkeys[2], (H,), jnp.float32, 0.5, 1.5)
    return jnp.stack([bias_row, rate_row, skip_row])


def adam_pair(key, shape):
    subkeys = jax.random.split(key, 2)
    first = 0.03 * jnp.clip(jax.random.normal(subkeys[0], shape, jnp.float32), -6.0, 6.0)
    second = jnp.exp(jax.random.uniform(subkeys[1], shape, jnp.float32, math.log(0.0001), math.log(0.01)))
    return jnp.stack([first, second])


def draw_adam_norm(key, part):
    return adam_pair(key, (D,))


def draw_adam_gate(key, part):
    return adam_pair(key, (E,))


def draw_adam_conv(key, part):
    return adam_pair(key, (K + 1, CONV_CH))


def draw_adam_head(key, part):
    return adam_pair(key, (3, H))


def block_levels(rng, dims, cuts, low, top_value):
    level = 1.0
    for dim, shards_of in cuts:
        draws = jax.random.uniform(jax.random.fold_in(jax.random.fold_in(rng, 6), dim), (shards_of,), jnp.float32, low / len(cuts), top_value / len(cuts))
        level = level * jnp.repeat(jnp.exp(draws), dims[dim] // shards_of).reshape((-1,) + (1,) * (len(dims) - 1 - dim))
    return level


def gaussian(rng, extent, width, bound, cuts=(), held_as=jnp.bfloat16):
    result = jax.random.normal(rng, extent, jnp.float32) * width
    if len(cuts) > 0:
        result = block_levels(rng, extent, cuts, -0.22, 0.18) * result
    return jnp.clip(result, min=-bound, max=bound).astype(held_as)


def setup_inputs(seed: int = 0) -> dict:
    seeds = jax.random.split(jax.random.key(seed), 17)
    return {
        "tokens": gaussian(seeds[0], (TOKENS, D), 1.0, 6.0, ((0, 32),)),
        "cotangent": gaussian(seeds[1], (TOKENS, D), 1.0, 6.0, ((0, 32),)),
        "block_fill": draw_block_fill(jax.random.fold_in(seeds[16], 71), 0),
        "block_start": draw_block_start(jax.random.fold_in(seeds[16], 71), 0),
        "in_weight": gaussian(seeds[4], (D, IN_COLS), D ** -0.5, 0.25, ((0, 4),), jnp.float32),
        "out_weight": gaussian(seeds[5], (E, D), E ** -0.5, 0.1875, ((0, 4),), jnp.float32),
        "in_moment": gaussian(seeds[6], (D, IN_COLS), 0.1, 1.5, ((0, 4),), jnp.float32),
        "out_moment": gaussian(seeds[7], (E, D), 0.3, 4.0, ((0, 4),), jnp.float32),
        "norm_gain": jnp.clip(1.0 + 0.1 * jax.random.normal(seeds[8], (D,), jnp.float32), 0.5, 1.5),
        "gate_gain": jnp.clip(1.0 + 0.1 * jax.random.normal(seeds[9], (E,), jnp.float32), 0.5, 1.5),
        "conv_params": jnp.clip(jax.random.uniform(seeds[10], (K + 1, CONV_CH), jnp.float32, -0.5, 0.5), -0.5, 0.5),
        "head_params": draw_head_params(jax.random.fold_in(seeds[16], 71), 0),
        "adam_norm": draw_adam_norm(jax.random.fold_in(seeds[16], 71), 0),
        "adam_gate": draw_adam_gate(jax.random.fold_in(seeds[16], 71), 0),
        "adam_conv": draw_adam_conv(jax.random.fold_in(seeds[16], 71), 0),
        "adam_head": draw_adam_head(jax.random.fold_in(seeds[16], 71), 0),
    }


highest_precision = lax.Precision.HIGHEST
norm_eps = 1e-05
schulz_coeffs = (3.4445, -4.775, 2.0315)
momentum_keep = 0.95
muon_rate = 0.05
adam_rate = 0.2
beta_first = 0.9
beta_second = 0.95
decay_rate = 0.1
adam_eps = 1e-08

def pre_norm(base, gain):
    return base * lax.rsqrt(lax.optimization_barrier(jnp.mean(base * base, -1, keepdims=True)) + norm_eps) * gain

def mixer(proj, conv_params, head_params, gate_gain, starts):
    total = proj.shape[0]
    blocks = starts.shape[0]
    length = total // blocks
    width_inner = gate_gain.shape[0]
    heads = head_params.shape[1]
    head_size = width_inner // heads
    taps = conv_params.shape[0] - 1
    channels = conv_params.shape[1]
    state_size = (channels - width_inner) // 2
    gate_in = proj[:, :width_inner]
    conv_in = proj[:, width_inner:width_inner + channels]
    dt_raw = proj[:, width_inner + channels:]
    seq_block = jnp.cumsum(starts).astype(jnp.int32)
    seq_token = jnp.repeat(seq_block, length).astype(jnp.int32)
    summed = conv_params[taps] + conv_params[taps - 1] * conv_in
    for offset in range(1, taps):
        moved = jnp.concatenate([jnp.zeros((offset, channels), jnp.float32), conv_in[:-offset]], 0)
        moved_seq = jnp.concatenate([jnp.full((offset,), -1, jnp.int32), seq_token[:-offset]], 0)
        same_seq = (moved_seq == seq_token).astype(jnp.float32)
        summed = summed + conv_params[taps - 1 - offset] * moved * same_seq[:, None]
    activated = jax.nn.silu(summed)
    values = activated[:, :width_inner].reshape(blocks, length, heads, head_size)
    b_input = activated[:, width_inner:width_inner + state_size].reshape(blocks, length, state_size)
    c_input = activated[:, width_inner + state_size:].reshape(blocks, length, state_size)
    step_size = jax.nn.softplus(dt_raw + head_params[0]).reshape(blocks, length, heads)
    rates = -jnp.exp(head_params[1])
    restart = starts.astype(jnp.float32)
    lower_mask = jnp.tril(jnp.ones((length, length), jnp.bool_))

    def advance(carry, items):
        block_vals, block_b, block_c, block_dt, fresh = items
        carry = carry * (1.0 - fresh)
        logs = jnp.cumsum(block_dt * rates, axis=0)
        columns = logs.T
        spread = columns[:, :, None] - columns[:, None, :]
        decay = jnp.where(lower_mask, jnp.exp(jnp.where(lower_mask, spread, 0.0)), 0.0)
        scores = jnp.dot(block_c, block_b.T, precision=highest_precision)
        weighted = block_vals * block_dt[:, :, None]
        local_out = jnp.einsum('hts,shp->thp', decay * scores[None], weighted, precision=highest_precision)
        carried = jnp.einsum('tn,hnp->thp', block_c, carry, precision=highest_precision) * jnp.exp(logs)[:, :, None]
        tail = jnp.exp(logs[-1][None, :] - logs)
        carry = carry * jnp.exp(logs[-1])[:, None, None] + jnp.einsum('sn,shp->hnp', block_b, weighted * tail[:, :, None], precision=highest_precision)
        return (carry, local_out + carried + head_params[2][None, :, None] * block_vals)
    initial = jnp.zeros((heads, state_size, head_size), jnp.float32)
    final_state, outputs = lax.scan(advance, initial, (values, b_input, c_input, step_size, restart))
    gated = outputs.reshape(total, width_inner) * jax.nn.silu(gate_in)
    return gated * lax.rsqrt(lax.optimization_barrier(jnp.mean(gated * gated, -1, keepdims=True)) + norm_eps) * gate_gain

def device_pass(tokens, cotangent, fill, starts, fwd_in, fwd_out, back_in, back_out, norm_gain, gate_gain, conv_params, head_params):
    total = tokens.shape[0]
    length = total // fill.shape[0]
    position = jnp.arange(total, dtype=jnp.int32) % length
    live = position < jnp.repeat(fill, length).astype(jnp.int32)
    base = tokens.astype(jnp.float32)
    normed, norm_back = jax.vjp(pre_norm, base, norm_gain)
    normed16 = normed.astype(jnp.bfloat16)
    proj = jnp.dot(normed16, fwd_in, preferred_element_type=jnp.float32)

    def mix_piece(proj_in, conv_in, head_in, gain_in):
        return mixer(proj_in, conv_in, head_in, gain_in, starts)
    mixed, mixer_back = jax.vjp(mix_piece, proj, conv_params, head_params, gate_gain)
    mixed16 = mixed.astype(jnp.bfloat16)
    branch = jnp.dot(mixed16, fwd_out, preferred_element_type=jnp.float32)
    activations = jnp.where(live[:, None], base + branch, 0.0).astype(jnp.bfloat16)
    live_cot = jnp.where(live[:, None], cotangent, jnp.zeros_like(cotangent))
    d_mixed = jnp.dot(live_cot, back_out.T, preferred_element_type=jnp.float32)
    grad_out = jnp.dot(mixed16.T, live_cot, preferred_element_type=jnp.float32)
    d_proj, grad_conv, grad_head, grad_gate = mixer_back(d_mixed)
    d_proj16 = d_proj.astype(jnp.bfloat16)
    grad_in = jnp.dot(normed16.T, d_proj16, preferred_element_type=jnp.float32)
    d_normed = jnp.dot(d_proj16, back_in.T, preferred_element_type=jnp.float32)
    d_base, grad_norm = norm_back(d_normed)
    input_grad = live_cot.astype(jnp.float32) + d_base
    return (activations, input_grad, grad_in, grad_out, grad_norm, grad_gate, grad_conv, grad_head)

def orthogonalize(matrix):
    frobenius = jnp.sqrt(jnp.sum(matrix * matrix))
    current = (matrix / (frobenius + 1e-07)).astype(jnp.bfloat16)
    flipped = matrix.shape[0] > matrix.shape[1]
    if flipped:
        current = current.T
    for turn in range(NS_STEPS):
        gram = jnp.dot(current, current.T, preferred_element_type=jnp.float32).astype(jnp.bfloat16)
        square = jnp.dot(gram, gram, preferred_element_type=jnp.float32)
        poly = (schulz_coeffs[1] * gram.astype(jnp.float32) + schulz_coeffs[2] * square).astype(jnp.bfloat16)
        current = (schulz_coeffs[0] * current.astype(jnp.float32) + jnp.dot(poly, current, preferred_element_type=jnp.float32)).astype(jnp.bfloat16)
    if flipped:
        current = current.T
    return current

def muon_apply(weight, orth, full_shape):
    factor = 0.2 * math.sqrt(max(full_shape[0], full_shape[1]))
    return weight - muon_rate * (factor * orth.astype(jnp.float32) + decay_rate * weight)

def adam_apply(param, grad, state):
    first = beta_first * state[0] + (1.0 - beta_first) * grad
    second = beta_second * state[1] + (1.0 - beta_second) * grad * grad
    first_hat = first / (1.0 - beta_first ** ADAM_STEP)
    second_hat = second / (1.0 - beta_second ** ADAM_STEP)
    updated = param - adam_rate * (first_hat / (jnp.sqrt(second_hat) + adam_eps) + decay_rate * param)
    return (updated, jnp.stack([first, second]))

def reference(tokens, cotangent, block_fill, block_start, in_weight, out_weight, in_moment, out_moment, norm_gain, gate_gain, conv_params, head_params, adam_norm, adam_gate, adam_conv, adam_head):
    devices = N_BLOCKS // BLOCKS_DEV
    in_half = in_weight.astype(jnp.bfloat16)
    out_half = out_weight.astype(jnp.bfloat16)
    tok_blocks = tokens.reshape(devices, TOK_DEV, D)
    cot_blocks = cotangent.reshape(devices, TOK_DEV, D)
    fill_blocks = block_fill.reshape(devices, BLOCKS_DEV)
    start_blocks = block_start.reshape(devices, BLOCKS_DEV)

    def one_device(carry, items):
        tok_here, cot_here, fill_here, start_here = items
        results = device_pass(tok_here, cot_here, fill_here, start_here, in_half, out_half, in_half, out_half, norm_gain, gate_gain, conv_params, head_params)
        carry = tuple((total + part for total, part in zip(carry, results[2:])))
        return (carry, (results[0], results[1]))
    zeros = (jnp.zeros((D, IN_COLS), jnp.float32), jnp.zeros((E, D), jnp.float32), jnp.zeros((D,), jnp.float32), jnp.zeros((E,), jnp.float32), jnp.zeros((K + 1, CONV_CH), jnp.float32), jnp.zeros((3, H), jnp.float32))
    sums, outputs = lax.scan(one_device, zeros, (tok_blocks, cot_blocks, fill_blocks, start_blocks))
    activations = outputs[0].reshape(TOKENS, D)
    input_grad = outputs[1].reshape(TOKENS, D)
    scale = 1.0 / math.sqrt(TOKENS)
    grad_in, grad_out, grad_norm, grad_gate, grad_conv, grad_head = [scale * part for part in sums]
    new_in_moment = momentum_keep * in_moment + grad_in
    new_out_moment = momentum_keep * out_moment + grad_out
    ranges = [(0, E), (E, 2 * E), (2 * E, IN_COLS)]
    new_pieces = []
    for lower, upper in ranges:
        orth = orthogonalize(new_in_moment[:, lower:upper])
        new_pieces.append(muon_apply(in_weight[:, lower:upper], orth, (D, upper - lower)))
    new_in_weight = jnp.concatenate(new_pieces, 1)
    new_out_weight = muon_apply(out_weight, orthogonalize(new_out_moment), (E, D))
    new_norm, state_norm = adam_apply(norm_gain, grad_norm, adam_norm)
    new_gate, state_gate = adam_apply(gate_gain, grad_gate, adam_gate)
    new_conv, state_conv = adam_apply(conv_params, grad_conv, adam_conv)
    new_head, state_head = adam_apply(head_params, grad_head, adam_head)
    return (activations, input_grad, grad_in, grad_out, grad_norm, grad_gate, grad_conv, grad_head, new_in_weight, new_out_weight, new_in_moment, new_out_moment, new_norm, new_gate, new_conv, new_head, state_norm, state_gate, state_conv, state_head)
```

```python
import functools
import math

import jax
import jax.numpy as jnp
from jax import lax
from jax.experimental import pallas as pl
from jax.experimental.pallas import tpu as pltpu
from jax.sharding import PartitionSpec as P

NS_STEPS = 5
ADAM_STEP = 3


ssd_precision = lax.Precision.HIGH
norm_eps = 1e-05
schulz_coeffs = (3.4445, -4.775, 2.0315)
momentum_keep = 0.95
muon_rate = 0.05
adam_rate = 0.2
beta_first = 0.9
beta_second = 0.95
decay_rate = 0.1
adam_eps = 1e-08


def pre_norm(base, gain):
    return base * lax.rsqrt(jnp.mean(base * base, -1, keepdims=True) + norm_eps) * gain


def mixer(proj, conv_params, head_params, gate_gain, starts):
    total = proj.shape[0]
    blocks = starts.shape[0]
    length = total // blocks
    width_inner = gate_gain.shape[0]
    heads = head_params.shape[1]
    head_size = width_inner // heads
    taps = conv_params.shape[0] - 1
    channels = conv_params.shape[1]
    state_size = (channels - width_inner) // 2
    gate_in = proj[:, :width_inner]
    conv_in = proj[:, width_inner : width_inner + channels]
    dt_raw = proj[:, width_inner + channels :]
    seq_block = jnp.cumsum(starts)
    seq_token = jnp.repeat(seq_block, length)
    summed = conv_params[taps] + conv_params[taps - 1] * conv_in
    for offset in range(1, taps):
        moved = jnp.concatenate([jnp.zeros((offset, channels), jnp.float32), conv_in[:-offset]], 0)
        moved_seq = jnp.concatenate([jnp.full((offset,), -1, jnp.int32), seq_token[:-offset]], 0)
        same_seq = (moved_seq == seq_token).astype(jnp.float32)
        summed = summed + conv_params[taps - 1 - offset] * moved * same_seq[:, None]
    activated = jax.nn.silu(summed)
    values = activated[:, :width_inner].reshape(total, heads, head_size)
    b_input = activated[:, width_inner : width_inner + state_size]
    c_input = activated[:, width_inner + state_size :]
    step_size = jax.nn.softplus(dt_raw + head_params[0])
    rates = -jnp.exp(head_params[1])
    lower = jnp.tril(jnp.ones((total, total), jnp.bool_))
    mask = jnp.logical_and(lower, seq_token[:, None] == seq_token[None, :])
    columns = jnp.einsum(
        "ts,sh->ht", lower.astype(jnp.float32), step_size * rates, precision=lax.Precision.HIGHEST
    )
    spread = columns[:, :, None] - columns[:, None, :]
    decay = jnp.where(mask, jnp.exp(jnp.where(mask, spread, 0.0)), 0.0)
    scores = jnp.dot(c_input, b_input.T, precision=ssd_precision)
    weighted = values * step_size[:, :, None]
    outputs = jnp.einsum(
        "hts,shp->thp", decay * scores[None], weighted, precision=ssd_precision
    )
    outputs = outputs + head_params[2][None, :, None] * values
    gated = outputs.reshape(total, width_inner) * jax.nn.silu(gate_in)
    return gated * lax.rsqrt(jnp.mean(gated * gated, -1, keepdims=True) + norm_eps) * gate_gain


def device_pass(
    tokens,
    cotangent,
    fill,
    starts,
    fwd_in,
    fwd_out,
    back_in,
    back_out,
    norm_gain,
    gate_gain,
    conv_params,
    head_params,
):
    total = tokens.shape[0]
    length = total // fill.shape[0]
    position = jnp.arange(total, dtype=jnp.int32) % length
    live = position < jnp.repeat(fill, length)
    base = tokens.astype(jnp.float32)
    normed, norm_back = jax.vjp(pre_norm, base, norm_gain)
    normed16 = normed.astype(jnp.bfloat16)
    proj = jnp.dot(normed16, fwd_in, preferred_element_type=jnp.float32)

    def mix_piece(proj_in, conv_in, head_in, gain_in):
        return mixer(proj_in, conv_in, head_in, gain_in, starts)

    mixed, mixer_back = jax.vjp(mix_piece, proj, conv_params, head_params, gate_gain)
    mixed16 = mixed.astype(jnp.bfloat16)
    branch = jnp.dot(mixed16, fwd_out, preferred_element_type=jnp.float32)
    activations = jnp.where(live[:, None], base + branch, 0.0).astype(jnp.bfloat16)
    live_cot = jnp.where(live[:, None], cotangent, jnp.zeros_like(cotangent))
    d_mixed = jnp.dot(live_cot, back_out.T, preferred_element_type=jnp.float32)
    grad_out = jnp.dot(mixed16.T, live_cot, preferred_element_type=jnp.float32)
    d_proj, grad_conv, grad_head, grad_gate = mixer_back(d_mixed)
    d_proj16 = d_proj.astype(jnp.bfloat16)
    grad_in = jnp.dot(normed16.T, d_proj16, preferred_element_type=jnp.float32)
    d_normed = jnp.dot(d_proj16, back_in.T, preferred_element_type=jnp.float32)
    d_base, grad_norm = norm_back(d_normed)
    input_grad = live_cot.astype(jnp.float32) + d_base
    return (activations, input_grad, grad_in, grad_out, grad_norm, grad_gate, grad_conv, grad_head)


def muon_apply(weight, orth, full_shape):
    factor = 0.2 * math.sqrt(max(full_shape[0], full_shape[1]))
    return weight - muon_rate * (factor * orth.astype(jnp.float32) + decay_rate * weight)


MESH = pl.DeviceIdType.MESH
LANES = 128


def places():
    rep = lax.axis_index("rep")
    shard = lax.axis_index("shard")
    core = lax.rem(rep, 2)
    chip = lax.div(rep, 2)
    chips = lax.axis_size("rep") // 2
    shards = lax.axis_size("shard")
    return rep, shard, core, chip, chips, shards


def line_order(shard, shards):
    tables = [
        sorted((z for z in range(shards) if z != here), key=lambda z: (abs(z - here), z))
        for here in range(shards)
    ]
    order = []
    for spot in range(shards - 1):
        value = jnp.int32(tables[0][spot])
        for here in range(1, shards):
            value = jnp.where(shard == here, jnp.int32(tables[here][spot]), value)
        order.append(value)
    return order


def plain_flips(chip, chips):
    count = chips.bit_length() - 1
    return [(1 << j) * (1 - 2 * lax.rem(lax.div(chip, 1 << j), 2)) for j in range(count)]


def core_flips(chip, core, chips):
    base = plain_flips(chip, chips)
    count = len(base)
    return [base[j] + core * (base[count - 1 - j] - base[j]) for j in range(count)]


def block_at(chip, flips, pattern):
    for j, step in enumerate(flips):
        if pattern >> j & 1:
            chip = chip + step
    return chip


def greet_peers(core, chip, shard, chips, shards):
    barrier = pltpu.get_barrier_semaphore()
    peers = [{"rep": 2 * chip + 1 - core}]
    for step in plain_flips(chip, chips):
        peers.append({"rep": 2 * (chip + step) + core})
    for step in range(1, shards):
        peers.append({"shard": lax.rem(shard + step, shards)})
    for peer in peers:
        pl.semaphore_signal(barrier, inc=1, device_id=peer, device_id_type=MESH)
    pl.semaphore_wait(barrier, len(peers))


def remote(src, dst, send, recv, peer):
    return pltpu.make_async_remote_copy(
        src_ref=src, dst_ref=dst, send_sem=send, recv_sem=recv, device_id=peer, device_id_type=MESH
    )


class Spread:
    def __init__(self, slot, sems, index):
        rep, shard, core, chip, chips, shards = places()
        self.slot = slot
        self.xs, self.xr, self.ps, self.pr = [
            (lambda q, s=s: s.at[tuple(index) + (q,)]) for s in sems
        ]
        self.chips, self.chip, self.core = chips, chip, core
        self.flips = core_flips(chip, core, chips)
        self.other_flips = core_flips(chip, 1 - core, chips)
        self.partner = {"rep": 2 * chip + 1 - core}

    def hops(self, pattern):
        ref = self.slot(block_at(self.chip, self.flips, pattern), self.core)
        copies = []
        for phase in range(pattern.bit_length(), len(self.flips)):
            q = pattern + (1 << phase)
            peer = {"rep": 2 * (self.chip + self.flips[phase]) + self.core}
            copies.append(remote(ref, ref, self.xs(q), self.xr(q), peer))
        copies.append(remote(ref, ref, self.ps(pattern), self.pr(pattern), self.partner))
        return copies

    def start(self, pattern):
        for copy in self.hops(pattern):
            copy.start()

    def wait(self, pattern):
        ref = self.slot(block_at(self.chip, self.flips, pattern), self.core)
        phase = pattern.bit_length() - 1
        peer = {"rep": 2 * (self.chip + self.flips[phase]) + self.core}
        remote(ref, ref, self.xs(pattern), self.xr(pattern), peer).wait_recv()

    def wait_partner(self):
        for pattern in range(self.chips):
            ref = self.slot(block_at(self.chip, self.other_flips, pattern), 1 - self.core)
            remote(ref, ref, self.ps(pattern), self.pr(pattern), self.partner).wait_recv()

    def wait_sends(self):
        for pattern in range(self.chips):
            for copy in self.hops(pattern):
                copy.wait_send()


def gather_kernel(in_ref, out_ref, all_in, all_out, send_in, send_out, zs, zr, xs, xr, ps, pr):
    rep, shard, core, chip, chips, shards = places()
    half = jnp.bfloat16
    triples = ((in_ref, send_in, all_in), (out_ref, send_out, all_out))
    for source, send, dst in triples:
        send[...] = source[chip, core].astype(half)
    greet_peers(core, chip, shard, chips, shards)
    order = line_order(shard, shards)
    started = []
    for a, (source, send, dst) in enumerate(triples):
        for other in reversed(order):
            copy = remote(
                send, dst.at[shard, chip, core], zs.at[a, other], zr.at[a, shard], {"shard": other}
            )
            copy.start()
            started.append(copy)
    for source, send, dst in triples:
        dst[shard] = source[...].astype(half)
    spreads = []
    for a, (source, send, dst) in enumerate(triples):
        for spot, other in enumerate(order):

            def slot(block, k, dst=dst, other=other):
                return dst.at[other, block, k]

            here = slot(chip, core)
            remote(here, here, zs.at[a, other], zr.at[a, other], {"shard": other}).wait_recv()
            spreads.append(Spread(slot, (xs, xr, ps, pr), (a, spot)))
            spreads[-1].start(0)
    for spread in spreads:
        for pattern in range(1, chips):
            spread.wait(pattern)
            spread.start(pattern)
    for spread in spreads:
        spread.wait_partner()
    for copy in started:
        copy.wait_send()
    for spread in spreads:
        spread.wait_sends()


def gather_rows(in_weight, out_weight):
    chips = lax.axis_size("rep") // 2
    shards = lax.axis_size("shard")
    half = jnp.bfloat16

    def split(rows):
        return rows.reshape(chips, 2, rows.shape[0] // (2 * chips), rows.shape[1])

    parts = [split(in_weight), split(out_weight)]
    vmem = pl.BlockSpec(memory_space=pltpu.VMEM)
    dma = pltpu.SemaphoreType.DMA
    whole = pl.pallas_call(
        gather_kernel,
        out_shape=[jax.ShapeDtypeStruct((shards,) + p.shape, half) for p in parts],
        in_specs=[vmem, vmem],
        out_specs=[vmem, vmem],
        scratch_shapes=[pltpu.VMEM(p.shape[2:], half) for p in parts]
        + [dma((2, shards))] * 2
        + [dma((2, shards, chips))] * 4,
        compiler_params=pltpu.CompilerParams(
            collective_id=0, has_side_effects=True, vmem_limit_bytes=60 * 1024 * 1024
        ),
    )(*parts)
    return [
        w.reshape(shards * p.shape[0], p.shape[1]) for w, p in zip(whole, (in_weight, out_weight))
    ]


def low_phase(pattern, phases):
    return phases if pattern == 0 else (pattern & -pattern).bit_length() - 1


def update_kernel(names, tail, gin, gout, small, inmom, outmom, *refs):
    k = dict(zip(names, refs))
    rep, shard, core, chip, chips, shards = places()
    f32 = jnp.float32
    half = jnp.bfloat16
    partner = {"rep": 2 * chip + 1 - core}
    flips = core_flips(chip, core, chips)
    other_flips = core_flips(chip, 1 - core, chips)
    base_flips = plain_flips(chip, chips)
    phases = len(flips)
    wide = k["gl"].shape[-1]
    thin = k["gt"].shape[-1]
    count = 4
    kinds = ("l", "l", "t", "o")
    offsets = (0, wide, 2 * wide)
    widths = (wide, wide, thin)
    owners = [number * shards // count for number in range(count)]
    order = (0, 1, 3, 2)
    line = line_order(shard, shards)
    started = []

    def go(copy):
        copy.start()
        started.append(copy)

    def source(number, block, which):
        if number == 3:
            return gout.at[:, :, block, which]
        return gin.at[:, block, which, :, pl.ds(offsets[number], widths[number])]

    local = [
        pltpu.make_async_copy(inmom.at[chip, core], k["momin"], k["lsem"].at[0]),
        pltpu.make_async_copy(outmom.at[:, chip, core], k["momout"], k["lsem"].at[1]),
    ]
    for copy in local:
        copy.start()
    greet_peers(core, chip, shard, chips, shards)
    stages = [
        sorted((d for d in range(1, chips) if low_phase(d, phases) == p), reverse=True)
        for p in range(phases)
    ] + [[0]]
    patterns = [d for stage in stages for d in stage]
    go(remote(small, k["tcore"], k["ts"].at[0], k["tr"].at[0], partner))
    for stage in ([0], range(1, phases + 1)):
        for number in order:
            for p in stage:
                for d in stages[p]:
                    go(
                        remote(
                            source(number, block_at(chip, other_flips, d), 1 - core),
                            k[f"first{number}"].at[d],
                            k["ds"].at[number, d], k["dr"].at[number, d], partner,
                        )
                    )
    for copy in local:
        copy.wait()
    k["momt"][...] = jnp.zeros(k["momt"].shape, f32)
    k["momt"][:, : tail] = k["momin"][:, 2 * wide :]

    def moment(number):
        if number == 3:
            return k["momout"]
        if number == 2:
            return k["momt"]
        return k["momin"].at[:, pl.ds(offsets[number], wide)]

    def send_moment(number):
        return remote(
            moment(number), k["momr" + kinds[number]].at[shard],
            k["ms"].at[number], k["mr"].at[shard], {"shard": owners[number]},
        )

    for number in range(count):

        @pl.when(shard != owners[number])
        def _():
            send_moment(number).start()

        @pl.when(shard == owners[number])
        def _():
            k["momr" + kinds[number]][shard] = moment(number)[...]

    def send_plane(number):
        return remote(
            k[f"sums{number}"].at[0], k["third" + kinds[number]].at[shard],
            k["zs"].at[number], k["zr"].at[shard], {"shard": owners[number]},
        )

    def reduce_step(number, d):
        last = low_phase(d, phases)
        slot = k[f"first{number}"].at[d]
        remote(slot, slot, k["ds"].at[number, d], k["dr"].at[number, d], partner).wait_recv()
        total = source(number, block_at(chip, flips, d), core)[...].astype(f32)
        total = total + slot[...].astype(f32)
        for q in range(last):
            came = d + (1 << q)
            slot = k[f"recv{number}"].at[came]
            peer = {"rep": 2 * (chip + flips[q]) + core}
            remote(slot, slot, k["rs"].at[number, came], k["rr"].at[number, came], peer).wait_recv()
            total = total + slot[...].astype(f32)
        k[f"sums{number}"][d] = total.astype(half)
        if d:
            peer = {"rep": 2 * (chip + flips[last]) + core}
            go(
                remote(
                    k[f"sums{number}"].at[d], k[f"recv{number}"].at[d],
                    k["rs"].at[number, d], k["rr"].at[number, d], peer,
                )
            )
        else:

            @pl.when(shard != owners[number])
            def _():
                send_plane(number).start()

            @pl.when(shard == owners[number])
            def _():
                k["third" + kinds[number]][shard] = k[f"sums{number}"][0]

    def small_step(j):
        if j == 0:
            remote(small, k["tcore"], k["ts"].at[0], k["tr"].at[0], partner).wait_recv()
            k["tacc"][0] = small[...] + k["tcore"][...]
        else:
            slot = k["trecv"].at[j - 1]
            peer = {"rep": 2 * (chip + base_flips[j - 1]) + core}
            remote(slot, slot, k["ts"].at[j], k["tr"].at[j], peer).wait_recv()
            k["tacc"][j] = k["tacc"][j - 1] + slot[...]
        if j < phases:
            peer = {"rep": 2 * (chip + base_flips[j]) + core}
            go(
                remote(
                    k["tacc"].at[j], k["trecv"].at[j], k["ts"].at[j + 1], k["tr"].at[j + 1], peer
                )
            )
        else:
            k["tz"][shard] = k["tacc"][phases]
            for other in line:
                go(
                    remote(
                        k["tacc"].at[phases], k["tz"].at[shard],
                        k["tzs"].at[other], k["tzr"].at[shard], {"shard": other},
                    )
                )

    for number in order:
        for d in stages[0]:
            reduce_step(number, d)
    small_step(0)
    steps = 1
    for turn in range(count + phases - 1):
        for p in range(1, phases + 1):
            spot = turn - (p - 1)
            if 0 <= spot < count:
                for d in stages[p]:
                    reduce_step(order[spot], d)
        if steps <= phases:
            small_step(steps)
            steps += 1

    def grad_slot(number):
        ref = k["g" + kinds[number]]
        if number == 3:
            return lambda block, which: ref.at[:, block, which]
        if number == 2:
            return lambda block, which: ref.at[block, which]
        return lambda block, which: ref.at[number, block, which]

    def orth_slot(number):
        ref = k["o" + kinds[number]]
        if number == 3:
            return lambda block, which: ref.at[:, block, which]
        if number == 2:
            return lambda block, which: ref.at[block, which]
        return lambda block, which: ref.at[number, block, which]

    grad_spreads = [
        Spread(grad_slot(number), [k["g" + s] for s in ("xs", "xr", "ps", "pr")], (number,))
        for number in range(count)
    ]
    orth_spreads = [
        Spread(orth_slot(number), [k["o" + s] for s in ("xs", "xr", "ps", "pr")], (number,))
        for number in range(count)
    ]

    def grads_first():
        for number in order:

            @pl.when(shard != owners[number])
            def _():
                slot = grad_slot(number)(chip, core)
                remote(
                    slot, slot, k["gzs"].at[0], k["gzr"].at[number], {"shard": owners[number]}
                ).wait_recv()

            grad_spreads[number].start(0)

    def grads_second():
        for pattern in range(1, chips):
            for number in order:
                grad_spreads[number].wait(pattern)
                grad_spreads[number].start(pattern)

    def hooks(turn):
        pl.when(turn == 1)(grads_first)
        pl.when(turn == 3)(grads_second)

    def finish_poly(gram, gram_ref, poly_ref):
        gram_ref[...] = gram.astype(half)
        gram = gram_ref[...]
        square = jnp.dot(gram, gram, preferred_element_type=f32)
        poly_ref[...] = (
            schulz_coeffs[1] * gram.astype(f32) + schulz_coeffs[2] * square
        ).astype(half)

    def iterate_left(cur, gram_ref, poly_ref):
        tall, across = cur.shape
        size = min(tall, across)

        @pl.loop(0, NS_STEPS)
        def _(turn):
            hooks(turn)
            now = cur[...]
            finish_poly(
                lax.dot_general(now, now, (((1,), (1,)), ((), ())), preferred_element_type=f32),
                gram_ref, poly_ref,
            )
            for q in range(across // size):
                part = cur[:, q * size : (q + 1) * size]
                cur[:, q * size : (q + 1) * size] = (
                    schulz_coeffs[0] * part.astype(f32)
                    + jnp.dot(poly_ref[...], part, preferred_element_type=f32)
                ).astype(half)

    def iterate_right(cur, gram_ref, poly_ref):
        tall, across = cur.shape
        size = math.gcd(tall, 512)

        @pl.loop(0, NS_STEPS)
        def _(turn):
            hooks(turn)
            gram = jnp.zeros((across, across), f32)
            for q in range(tall // size):
                part = cur[q * size : (q + 1) * size]
                gram = gram + lax.dot_general(
                    part, part, (((0,), (0,)), ((), ())), preferred_element_type=f32
                )
            finish_poly(gram, gram_ref, poly_ref)
            for q in range(tall // size):
                part = cur[q * size : (q + 1) * size]
                cur[q * size : (q + 1) * size] = (
                    schulz_coeffs[0] * part.astype(f32)
                    + jnp.dot(part, poly_ref[...], preferred_element_type=f32)
                ).astype(half)

    def own_work(kind, number):
        third, momr, buf, cur = [k[name + kind] for name in ("third", "momr", "buf", "cur")]
        gsend = k["gsend" + kind]
        folded = kind == "o"

        def piece(block, which):
            return buf.at[:, :, block, which] if folded else buf.at[:, block, which]

        def rows(ref, block, which):
            if kind == "l":
                return ref.at[number, block, which]
            return ref.at[:, block, which] if folded else ref.at[block, which]

        for other in line:
            slot = third.at[other]
            remote(slot, slot, k["zs"].at[0], k["zr"].at[other], {"shard": other}).wait_recv()
            slot = momr.at[other]
            remote(slot, slot, k["ms"].at[0], k["mr"].at[other], {"shard": other}).wait_recv()
        total = third[0].astype(f32)
        for z in range(1, shards):
            total = total + third[z].astype(f32)
        merged = (momentum_keep * momr[...] + total).astype(half)
        if folded:
            buf[:, :, chip, core] = merged
        else:
            buf[:, chip, core] = merged
        spread = Spread(piece, [k["b" + s] for s in ("xs", "xr", "ps", "pr")], ())
        spread.start(0)
        gsend[...] = total.astype(half)

        def send_grad(other):
            return remote(
                gsend.at[other], rows(k["g" + kind], chip, core),
                k["gzs"].at[other], k["gzr"].at[number], {"shard": other},
            )

        for other in line:
            send_grad(other).start()
        rows(k["g" + kind], chip, core)[...] = gsend[shard]
        for pattern in range(1, chips):
            spread.wait(pattern)
            spread.start(pattern)
        spread.wait_partner()
        matrix = buf[...].reshape(cur.shape).astype(f32)
        frobenius = jnp.sqrt(jnp.sum(matrix * matrix))
        cur[...] = (matrix / (frobenius + 1e-07)).astype(half)
        if kind == "l":
            iterate_left(cur, k["graml"], k["polyl"])
        else:
            iterate_right(cur, k["gram" + kind], k["poly" + kind])
        spread.wait_sends()
        buf[...] = cur[...].reshape(buf.shape)

        def back(other):
            part = buf.at[other]
            part = part.at[:, chip, core] if folded else part.at[chip, core]
            return remote(
                part, rows(k["o" + kind], chip, core),
                k["ozs"].at[other], k["ozr"].at[number], {"shard": other},
            )

        for other in line:
            back(other).start()
        if kind == "l":
            k["ol"][number] = buf[shard]
        else:
            k["o" + kind][...] = buf[shard]
        for other in line:
            send_grad(other).wait_send()
            back(other).wait_send()

    def is_owner(numbers):
        flag = shard == owners[numbers[0]]
        for number in numbers[1:]:
            flag = jnp.logical_or(flag, shard == owners[number])
        return flag

    pl.when(is_owner((0, 1)))(lambda: own_work("l", lax.div(shard * count, shards)))
    pl.when(is_owner((2,)))(lambda: own_work("t", 2))
    pl.when(is_owner((3,)))(lambda: own_work("o", 3))
    if shards > count:

        @pl.when(jnp.logical_not(is_owner(range(count))))
        def _():
            grads_first()
            grads_second()

    back_order = (2, 0, 1, 3)
    for number in back_order:

        @pl.when(shard != owners[number])
        def _():
            slot = orth_slot(number)(chip, core)
            remote(
                slot, slot, k["ozs"].at[0], k["ozr"].at[number], {"shard": owners[number]}
            ).wait_recv()
            orth_spreads[number].start(0)

    for other in line:
        slot = k["tz"].at[other]
        remote(slot, slot, k["tzs"].at[other], k["tzr"].at[other], {"shard": other}).wait_recv()
    total = k["tz"][0]
    for z in range(1, shards):
        total = total + k["tz"][z]
    k["ftiny"][...] = total
    for spread in grad_spreads:
        spread.wait_partner()
    for number in back_order:

        @pl.when(shard != owners[number])
        def _():
            for pattern in range(1, chips):
                orth_spreads[number].wait(pattern)
                orth_spreads[number].start(pattern)

    for copy in started:
        copy.wait_send()
    for number in range(count):

        @pl.when(shard != owners[number])
        def _():
            send_moment(number).wait_send()
            send_plane(number).wait_send()

        grad_spreads[number].wait_sends()
    for number in back_order:

        @pl.when(shard != owners[number])
        def _():
            orth_spreads[number].wait_partner()
            orth_spreads[number].wait_sends()


def reduce_and_orthogonalize(grad_in, grad_out, small, in_moment, out_moment, wide):
    chips = lax.axis_size("rep") // 2
    shards = lax.axis_size("shard")
    half = jnp.bfloat16
    f32 = jnp.float32
    height, columns = grad_in.shape
    depth = grad_out.shape[1]
    rows = height // (shards * chips * 2)
    folds = grad_out.shape[0] // height
    tail = columns - 2 * wide
    thin = -(-tail // LANES) * LANES
    gin = jnp.pad(grad_in, ((0, 0), (0, thin - tail))).reshape(
        shards, chips, 2, rows, 2 * wide + thin
    )
    gout = grad_out.reshape(shards, folds, chips, 2, rows, depth)
    inmom = in_moment.reshape(chips, 2, rows, columns)
    outmom = out_moment.reshape(folds, chips, 2, rows, depth)
    outs = {
        "gl": ((2, chips, 2, rows, wide), half),
        "gt": ((chips, 2, rows, thin), half),
        "go": ((folds, chips, 2, rows, depth), half),
        "ol": ((2, chips, 2, rows, wide), half),
        "ot": ((chips, 2, rows, thin), half),
        "oo": ((folds, chips, 2, rows, depth), half),
        "ftiny": (small.shape, f32),
    }
    tails = [(rows, wide), (rows, wide), (rows, thin), (folds, rows, depth)]
    scratch = {
        "momin": ((rows, columns), f32),
        "momout": ((folds, rows, depth), f32),
        "momt": ((rows, thin), f32),
        "tcore": (small.shape, f32),
        "tacc": ((chips.bit_length(),) + small.shape, f32),
        "trecv": ((chips.bit_length(),) + small.shape, f32),
        "tz": ((shards,) + small.shape, f32),
    }
    for number, part in enumerate(tails):
        for name in ("first", "sums", "recv"):
            scratch[f"{name}{number}"] = ((chips, shards) + part, half)
    full = {
        "l": ((shards, chips, 2, rows, wide), (height, wide), height),
        "t": ((shards, chips, 2, rows, thin), (height, thin), thin),
        "o": ((shards, folds, chips, 2, rows, depth), (height * folds, depth), depth),
    }
    for kind, number in (("l", 0), ("t", 2), ("o", 3)):
        scratch["third" + kind] = ((shards, shards) + tails[number], half)
        scratch["momr" + kind] = ((shards,) + tails[number], f32)
        scratch["gsend" + kind] = ((shards,) + tails[number], half)
        scratch["buf" + kind] = (full[kind][0], half)
        scratch["cur" + kind] = (full[kind][1], half)
        scratch["gram" + kind] = ((full[kind][2],) * 2, half)
        scratch["poly" + kind] = ((full[kind][2],) * 2, half)
    sems = {
        "lsem": (2,),
        "ts": (chips.bit_length(),),
        "tr": (chips.bit_length(),),
        "tzs": (shards,),
        "tzr": (shards,),
        "zs": (4,),
        "zr": (shards,),
        "ms": (4,),
        "mr": (shards,),
        "gzs": (shards,),
        "gzr": (4,),
        "ozs": (shards,),
        "ozr": (4,),
    }
    for name in ("ds", "dr", "rs", "rr"):
        sems[name] = (4, chips)
    for name in ("xs", "xr", "ps", "pr"):
        sems["b" + name] = (chips,)
        sems["g" + name] = (4, chips)
        sems["o" + name] = (4, chips)
    vmem = pl.BlockSpec(memory_space=pltpu.VMEM)
    anywhere = pl.BlockSpec(memory_space=pl.ANY)
    names = list(outs) + list(scratch) + list(sems)
    return pl.pallas_call(
        functools.partial(update_kernel, names, tail),
        out_shape=[jax.ShapeDtypeStruct(s, d) for s, d in outs.values()],
        in_specs=[vmem] * 3 + [anywhere] * 2,
        out_specs=[vmem] * len(outs),
        scratch_shapes=[pltpu.VMEM(s, d) for s, d in scratch.values()]
        + [pltpu.SemaphoreType.DMA(s) for s in sems.values()],
        compiler_params=pltpu.CompilerParams(
            collective_id=1, has_side_effects=True, vmem_limit_bytes=60 * 1024 * 1024
        ),
    )(gin, gout, small, inmom, outmom)


def finish_kernel(
    sizes, gl, gt, go, ol, ot, oo, tiny, in_w, out_w, in_m, out_m,
    p_norm, p_gate, p_conv, p_head, a_norm, a_gate, a_conv, a_head,
    grad_in, grad_out, grad_norm, grad_gate, grad_conv, grad_head,
    new_in, new_out, mom_in, mom_out,
    n_norm, n_gate, n_conv, n_head, s_norm, s_gate, s_conv, s_head,
):
    f32 = jnp.float32
    wide = gl.shape[-1]
    tail = in_w.shape[1] - 2 * wide
    spans = ((0, wide), (wide, wide), (2 * wide, tail))
    for number, (low, width) in enumerate(spans):
        if number < 2:
            grad, orth = gl[number].astype(f32), ol[number].astype(f32)
        else:
            grad, orth = gt[:, :width].astype(f32), ot[:, :width].astype(f32)
        here = slice(low, low + width)
        grad_in[:, here] = grad
        mom_in[:, here] = momentum_keep * in_m[:, here] + grad
        new_in[:, here] = muon_apply(in_w[:, here], orth, sizes[number])
    grad = go[...].astype(f32)
    grad_out[...] = grad
    mom_out[...] = momentum_keep * out_m[...] + grad
    new_out[...] = muon_apply(out_w[...], oo[...].astype(f32), sizes[3])

    def adam(grad, param, state):
        first = beta_first * state[0] + (1.0 - beta_first) * grad
        second = beta_second * state[1] + (1.0 - beta_second) * grad * grad
        first_hat = first / (1.0 - beta_first**ADAM_STEP)
        second_hat = second / (1.0 - beta_second**ADAM_STEP)
        updated = param - adam_rate * (
            first_hat / (jnp.sqrt(second_hat) + adam_eps) + decay_rate * param
        )
        return updated, first, second

    taps = p_conv.shape[0]
    conv = tiny[:taps]
    grad_conv[...] = conv
    n_conv[...], s_conv[0], s_conv[1] = adam(conv, p_conv[...], (a_conv[0], a_conv[1]))
    for row, grad_ref, p, a, n, s in (
        (taps, grad_gate, p_gate, a_gate, n_gate, s_gate),
        (taps + 1, grad_norm, p_norm, a_norm, n_norm, s_norm),
    ):
        grad = tiny[row : row + 1, : p.shape[1]]
        grad_ref[...] = grad
        n[...], s[0:1], s[1:2] = adam(grad, p[...], (a[0:1], a[1:2]))
    heads = p_head.shape[1]
    for i in range(p_head.shape[0]):
        grad = tiny[taps + 2 : taps + 3, i * LANES : i * LANES + heads]
        one = slice(i, i + 1)
        grad_head[one] = grad
        n_head[one], s_head[0, one], s_head[1, one] = adam(
            grad, p_head[one], (a_head[0, one], a_head[1, one])
        )


def pack_small(grad_norm, grad_gate, grad_conv, grad_head):
    width = grad_conv.shape[1]

    def fit(row):
        return jnp.pad(row, ((0, 0), (0, width - row.shape[1])))

    heads = [jnp.pad(grad_head[i][None], ((0, 0), (0, LANES - grad_head.shape[1]))) for i in range(3)]
    packed = jnp.concatenate(
        [grad_conv, fit(grad_gate[None]), fit(grad_norm[None]), fit(jnp.concatenate(heads, 1))], 0
    )
    return jnp.pad(packed, ((0, -packed.shape[0] % 8), (0, 0)))


def local(
    tokens,
    cotangent,
    block_fill,
    block_start,
    in_weight,
    out_weight,
    in_moment,
    out_moment,
    norm_gain,
    gate_gain,
    conv_params,
    head_params,
    adam_norm,
    adam_gate,
    adam_conv,
    adam_head,
):
    shards = lax.axis_size("shard")
    replicas = lax.axis_size("rep")
    whole_in, whole_out = gather_rows(in_weight, out_weight)
    results = device_pass(
        tokens,
        cotangent,
        block_fill,
        block_start,
        whole_in,
        whole_out,
        whole_in,
        whole_out,
        norm_gain,
        gate_gain,
        conv_params,
        head_params,
    )
    activations, input_grad, grad_in, grad_out, grad_norm, grad_gate, grad_conv, grad_head = results
    scale = 1.0 / math.sqrt(tokens.shape[0] * shards * replicas)
    wide = gate_gain.shape[0]
    gl, gt, go, ol, ot, oo, tiny = reduce_and_orthogonalize(
        (scale * grad_in).astype(jnp.bfloat16),
        (scale * grad_out).astype(jnp.bfloat16),
        scale * pack_small(grad_norm, grad_gate, grad_conv, grad_head),
        in_moment,
        out_moment,
        wide,
    )
    rows = in_weight.shape[0]
    tail = in_weight.shape[1] - 2 * wide
    sizes = (
        (rows * shards, wide),
        (rows * shards, wide),
        (rows * shards, tail),
        (out_weight.shape[0] * shards, out_weight.shape[1]),
    )
    pieces = []
    for l, t, o in ((gl, gt, go), (ol, ot, oo)):
        pieces += [l.reshape(2, rows, wide), t.reshape(rows, -1), o.reshape(out_weight.shape)]
    params = [norm_gain[None], gate_gain[None], conv_params, head_params]
    states = [adam_norm, adam_gate, adam_conv, adam_head]
    like = [in_weight, out_weight] + params + [in_weight, out_weight] * 2 + params + states
    vmem = pl.BlockSpec(memory_space=pltpu.VMEM)
    done = pl.pallas_call(
        functools.partial(finish_kernel, sizes),
        out_shape=[jax.ShapeDtypeStruct(a.shape, a.dtype) for a in like],
        in_specs=[vmem] * (11 + 8),
        out_specs=[vmem] * len(like),
        compiler_params=pltpu.CompilerParams(vmem_limit_bytes=60 * 1024 * 1024),
    )(*pieces, tiny, in_weight, out_weight, in_moment, out_moment, *params, *states)
    done = list(done)
    for spot, gain in ((2, norm_gain), (3, gate_gain), (10, norm_gain), (11, gate_gain)):
        done[spot] = done[spot].reshape(gain.shape)
    return (activations, input_grad, *done)


def solution(mesh):
    return jax.shard_map(
        local,
        mesh=mesh,
        in_specs=(
            P(("rep", "shard"), None),
            P(("rep", "shard"), None),
            P(("rep", "shard")),
            P(("rep", "shard")),
            P("shard", None),
            P("shard", None),
            P("shard", None),
            P("shard", None),
            P(),
            P(),
            P(),
            P(),
            P(),
            P(),
            P(),
            P(),
        ),
        out_specs=(
            P(("rep", "shard"), None),
            P(("rep", "shard"), None),
            P("shard", None),
            P("shard", None),
            P(),
            P(),
            P(),
            P(),
            P("shard", None),
            P("shard", None),
            P("shard", None),
            P("shard", None),
            P(),
            P(),
            P(),
            P(),
            P(),
            P(),
            P(),
            P(),
        ),
        check_vma=False,
    )
```

```python
import functools
import math

import jax
import jax.numpy as jnp
from jax import lax
from jax.experimental import pallas as pl
from jax.experimental.pallas import tpu as pltpu
from jax.sharding import PartitionSpec as P

NS_STEPS = 5
ADAM_STEP = 3


ssd_precision = lax.Precision.HIGH
norm_eps = 1e-05
schulz_coeffs = (3.4445, -4.775, 2.0315)
momentum_keep = 0.95
muon_rate = 0.05
adam_rate = 0.2
beta_first = 0.9
beta_second = 0.95
decay_rate = 0.1
adam_eps = 1e-08


def pre_norm(base, gain):
    return base * lax.rsqrt(jnp.mean(base * base, -1, keepdims=True) + norm_eps) * gain


def mixer(proj, conv_params, head_params, gate_gain, starts):
    total = proj.shape[0]
    blocks = starts.shape[0]
    length = total // blocks
    width_inner = gate_gain.shape[0]
    heads = head_params.shape[1]
    head_size = width_inner // heads
    taps = conv_params.shape[0] - 1
    channels = conv_params.shape[1]
    state_size = (channels - width_inner) // 2
    gate_in = proj[:, :width_inner]
    conv_in = proj[:, width_inner : width_inner + channels]
    dt_raw = proj[:, width_inner + channels :]
    seq_block = jnp.cumsum(starts)
    seq_token = jnp.repeat(seq_block, length)
    summed = conv_params[taps] + conv_params[taps - 1] * conv_in
    for offset in range(1, taps):
        moved = jnp.concatenate([jnp.zeros((offset, channels), jnp.float32), conv_in[:-offset]], 0)
        moved_seq = jnp.concatenate([jnp.full((offset,), -1, jnp.int32), seq_token[:-offset]], 0)
        same_seq = (moved_seq == seq_token).astype(jnp.float32)
        summed = summed + conv_params[taps - 1 - offset] * moved * same_seq[:, None]
    activated = jax.nn.silu(summed)
    values = activated[:, :width_inner].reshape(total, heads, head_size)
    b_input = activated[:, width_inner : width_inner + state_size]
    c_input = activated[:, width_inner + state_size :]
    step_size = jax.nn.softplus(dt_raw + head_params[0])
    rates = -jnp.exp(head_params[1])
    lower = jnp.tril(jnp.ones((total, total), jnp.bool_))
    mask = jnp.logical_and(lower, seq_token[:, None] == seq_token[None, :])
    columns = jnp.einsum(
        "ts,sh->ht", lower.astype(jnp.float32), step_size * rates, precision=lax.Precision.HIGHEST
    )
    spread = columns[:, :, None] - columns[:, None, :]
    decay = jnp.where(mask, jnp.exp(jnp.where(mask, spread, 0.0)), 0.0)
    scores = jnp.dot(c_input, b_input.T, precision=ssd_precision)
    weighted = values * step_size[:, :, None]
    outputs = jnp.einsum(
        "hts,shp->thp", decay * scores[None], weighted, precision=ssd_precision
    )
    outputs = outputs + head_params[2][None, :, None] * values
    gated = outputs.reshape(total, width_inner) * jax.nn.silu(gate_in)
    return gated * lax.rsqrt(jnp.mean(gated * gated, -1, keepdims=True) + norm_eps) * gate_gain


def device_pass(
    tokens,
    cotangent,
    fill,
    starts,
    fwd_in,
    fwd_out,
    back_in,
    back_out,
    norm_gain,
    gate_gain,
    conv_params,
    head_params,
):
    total = tokens.shape[0]
    length = total // fill.shape[0]
    position = jnp.arange(total, dtype=jnp.int32) % length
    live = position < jnp.repeat(fill, length)
    base = tokens.astype(jnp.float32)
    normed, norm_back = jax.vjp(pre_norm, base, norm_gain)
    normed16 = normed.astype(jnp.bfloat16)
    proj = jnp.dot(normed16, fwd_in, preferred_element_type=jnp.float32)

    def mix_piece(proj_in, conv_in, head_in, gain_in):
        return mixer(proj_in, conv_in, head_in, gain_in, starts)

    mixed, mixer_back = jax.vjp(mix_piece, proj, conv_params, head_params, gate_gain)
    mixed16 = mixed.astype(jnp.bfloat16)
    branch = jnp.dot(mixed16, fwd_out, preferred_element_type=jnp.float32)
    activations = jnp.where(live[:, None], base + branch, 0.0).astype(jnp.bfloat16)
    live_cot = jnp.where(live[:, None], cotangent, jnp.zeros_like(cotangent))
    d_mixed = jnp.dot(live_cot, back_out.T, preferred_element_type=jnp.float32)
    d_proj, grad_conv, grad_head, grad_gate = mixer_back(d_mixed)
    d_proj16 = d_proj.astype(jnp.bfloat16)
    d_normed = jnp.dot(d_proj16, back_in.T, preferred_element_type=jnp.float32)
    d_base, grad_norm = norm_back(d_normed)
    input_grad = live_cot.astype(jnp.float32) + d_base
    factors = (normed16, d_proj16, mixed16, live_cot)
    return (activations, input_grad, factors, grad_norm, grad_gate, grad_conv, grad_head)


def muon_apply(weight, orth, full_shape):
    factor = 0.2 * math.sqrt(max(full_shape[0], full_shape[1]))
    return weight - muon_rate * (factor * orth.astype(jnp.float32) + decay_rate * weight)


MESH = pl.DeviceIdType.MESH
LANES = 128


def places():
    rep = lax.axis_index("rep")
    shard = lax.axis_index("shard")
    core = lax.rem(rep, 2)
    chip = lax.div(rep, 2)
    chips = lax.axis_size("rep") // 2
    shards = lax.axis_size("shard")
    return rep, shard, core, chip, chips, shards


def line_order(shard, shards):
    tables = [
        sorted((z for z in range(shards) if z != here), key=lambda z: (abs(z - here), z))
        for here in range(shards)
    ]
    order = []
    for spot in range(shards - 1):
        value = jnp.int32(tables[0][spot])
        for here in range(1, shards):
            value = jnp.where(shard == here, jnp.int32(tables[here][spot]), value)
        order.append(value)
    return order


def plain_flips(chip, chips):
    count = chips.bit_length() - 1
    return [(1 << j) * (1 - 2 * lax.rem(lax.div(chip, 1 << j), 2)) for j in range(count)]


def turned_flips(chip, chips, turned):
    flips = plain_flips(chip, chips)
    return flips[::-1] if turned else flips


def block_at(chip, flips, pattern):
    for j, step in enumerate(flips):
        if pattern >> j & 1:
            chip = chip + step
    return chip


def greet_peers(core, chip, shard, chips, shards):
    barrier = pltpu.get_barrier_semaphore()
    peers = [{"rep": 2 * chip + 1 - core}]
    for step in plain_flips(chip, chips):
        peers.append({"rep": 2 * (chip + step) + core})
    for step in range(1, shards):
        peers.append({"shard": lax.rem(shard + step, shards)})
    for peer in peers:
        pl.semaphore_signal(barrier, inc=1, device_id=peer, device_id_type=MESH)
    pl.semaphore_wait(barrier, len(peers))


def remote(src, dst, send, recv, peer):
    return pltpu.make_async_remote_copy(
        src_ref=src, dst_ref=dst, send_sem=send, recv_sem=recv, device_id=peer, device_id_type=MESH
    )


class Spread:
    def __init__(self, slot, sems, index, turned):
        rep, shard, core, chip, chips, shards = places()
        self.slot = slot
        self.xs, self.xr, self.ps, self.pr = [
            (lambda q, s=s: s.at[tuple(index) + (q,)]) for s in sems
        ]
        self.chips, self.chip, self.core = chips, chip, core
        self.flips = turned_flips(chip, chips, turned)
        self.partner = {"rep": 2 * chip + 1 - core}

    def hops(self, pattern):
        ref = self.slot(block_at(self.chip, self.flips, pattern), self.core)
        copies = []
        for phase in range(pattern.bit_length(), len(self.flips)):
            q = pattern + (1 << phase)
            peer = {"rep": 2 * (self.chip + self.flips[phase]) + self.core}
            copies.append(remote(ref, ref, self.xs(q), self.xr(q), peer))
        copies.append(remote(ref, ref, self.ps(pattern), self.pr(pattern), self.partner))
        return copies

    def start(self, pattern):
        for copy in self.hops(pattern):
            copy.start()

    def wait(self, pattern):
        ref = self.slot(block_at(self.chip, self.flips, pattern), self.core)
        phase = pattern.bit_length() - 1
        peer = {"rep": 2 * (self.chip + self.flips[phase]) + self.core}
        remote(ref, ref, self.xs(pattern), self.xr(pattern), peer).wait_recv()

    def wait_partner(self):
        for pattern in range(self.chips):
            ref = self.slot(block_at(self.chip, self.flips, pattern), 1 - self.core)
            remote(ref, ref, self.ps(pattern), self.pr(pattern), self.partner).wait_recv()

    def wait_sends(self):
        for pattern in range(self.chips):
            for copy in self.hops(pattern):
                copy.wait_send()


def gather_kernel(
    in_ref, out_ref, mom_ref, all_in, all_out, mom_rows,
    flat_in, send_in, send_out, zs, zr, xs, xr, ps, pr,
):
    rep, shard, core, chip, chips, shards = places()
    half = jnp.bfloat16
    rows = flat_in.shape[1]
    turned = in_ref[...].T
    for j in range(2 * chips):
        flat_in[j] = turned[j * rows : (j + 1) * rows]
    send_in[...] = flat_in[2 * chip + core].astype(half)
    send_out[...] = out_ref[chip, core].astype(half)
    greet_peers(core, chip, shard, chips, shards)
    pairs = ((send_in, all_in), (send_out, all_out))

    def hop(a, origin, src, sign):
        return remote(
            src, pairs[a][1].at[origin, chip, core],
            zs.at[a, origin, (sign + 1) // 2], zr.at[a, origin], {"shard": shard + sign},
        )

    def room(sign):
        return shard + 1 < shards if sign > 0 else shard > 0

    for a, (send, dst) in enumerate(pairs):
        for sign in (1, -1):

            @pl.when(room(sign))
            def _():
                hop(a, shard, send, sign).start()

    for j in range(2 * chips):
        all_in[shard, j // 2, j % 2] = flat_in[j].astype(half)
    all_out[shard] = out_ref[...].astype(half)
    moment = mom_ref[...].T
    for j in range(2 * chips):
        mom_rows[j] = moment[j * rows : (j + 1) * rows]

    def far(step, sign):
        origin = shard - sign * step
        held = origin >= 0 if sign > 0 else origin < shards
        return origin, held

    visits = [
        (a, step, sign)
        for a in range(2)
        for step in range(1, shards)
        for sign in (1, -1)
    ]

    def spread_of(a, step, sign):
        origin, held = far(step, sign)
        dst = pairs[a][1]
        sems = [ref for ref in (xs, xr, ps, pr)]
        odd = (step + (sign > 0) + a) % 2 == 1
        return Spread(lambda block, k: dst.at[origin, block, k], sems, (a, origin), odd), held

    for a, step, sign in visits:
        origin, held = far(step, sign)

        @pl.when(held)
        def _():
            slot = pairs[a][1].at[origin, chip, core]
            hop(a, origin, slot, sign).wait_recv()

            @pl.when(room(sign))
            def _():
                hop(a, origin, slot, sign).start()

            spread_of(a, step, sign)[0].start(0)

    for pattern in range(1, chips):
        for a, step, sign in visits:
            spread, held = spread_of(a, step, sign)

            @pl.when(held)
            def _():
                spread.wait(pattern)
                spread.start(pattern)

    for a, step, sign in visits:
        origin, held = far(step, sign)

        @pl.when(held)
        def _():
            spread = spread_of(a, step, sign)[0]
            spread.wait_partner()
            spread.wait_sends()

            @pl.when(room(sign))
            def _():
                hop(a, origin, pairs[a][1].at[origin, chip, core], sign).wait_send()

    for a, (send, dst) in enumerate(pairs):
        for sign in (1, -1):

            @pl.when(room(sign))
            def _():
                hop(a, shard, send, sign).wait_send()


def gather_rows(in_weight, out_weight, in_moment):
    chips = lax.axis_size("rep") // 2
    shards = lax.axis_size("shard")
    half = jnp.bfloat16
    f32 = jnp.float32
    height, columns = in_weight.shape
    rows = height // (2 * chips)
    depth = out_weight.shape[1]
    out_rows = out_weight.shape[0] // (2 * chips)
    vmem = pl.BlockSpec(memory_space=pltpu.VMEM)
    dma = pltpu.SemaphoreType.DMA
    whole_in, whole_out, moment = pl.pallas_call(
        gather_kernel,
        out_shape=[
            jax.ShapeDtypeStruct((shards, chips, 2, rows, columns), half),
            jax.ShapeDtypeStruct((shards, chips, 2, out_rows, depth), half),
            jax.ShapeDtypeStruct((2 * chips, rows, columns), f32),
        ],
        in_specs=[vmem] * 3,
        out_specs=[vmem] * 3,
        scratch_shapes=[
            pltpu.VMEM((2 * chips, rows, columns), f32),
            pltpu.VMEM((rows, columns), half),
            pltpu.VMEM((out_rows, depth), half),
            dma((2, shards, 2)),
            dma((2, shards)),
        ]
        + [dma((2, shards, chips))] * 4,
        compiler_params=pltpu.CompilerParams(
            collective_id=0, has_side_effects=True, vmem_limit_bytes=60 * 1024 * 1024
        ),
    )(in_weight.T, out_weight.reshape(chips, 2, out_rows, depth), in_moment.T)
    return (
        whole_in.reshape(shards * height, columns),
        whole_out.reshape(shards * out_weight.shape[0], depth),
        moment.reshape(chips, 2, rows, columns),
    )


def low_phase(pattern, phases):
    return phases if pattern == 0 else (pattern & -pattern).bit_length() - 1


def update_kernel(names, tail, scale, normed, dproj, mixed, livecot, small, inmom, outmom, *refs):
    k = dict(zip(names, refs))
    rep, shard, core, chip, chips, shards = places()
    f32 = jnp.float32
    half = jnp.bfloat16
    partner = {"rep": 2 * chip + 1 - core}
    base_flips = plain_flips(chip, chips)
    phases = len(base_flips)
    turned = (False, True, True, False)
    wide = k["gl"].shape[-1]
    thin = k["gt"].shape[-1]
    count = 4
    kinds = ("l", "l", "t", "o")
    offsets = (0, wide, 2 * wide)
    widths = (wide, wide, thin)
    owners = [number * shards // count for number in range(count)]
    order = (3, 0, 1, 2)
    line = line_order(shard, shards)
    started = []

    def go(copy):
        copy.start()
        started.append(copy)

    def source(number, block, which):
        ref = k[f"grad{number}"]
        return ref.at[:, :, block, which] if number == 3 else ref.at[:, block, which]

    def flips_of(number):
        return turned_flips(chip, chips, turned[number])

    def own_grad(number):
        ref = k[f"grad{number}"]
        first, second = (mixed, livecot) if number == 3 else (normed, dproj)
        second = second[...]
        if number < 3:
            second = second[:, offsets[number] : offsets[number] + (tail if number == 2 else wide)]
        value = lax.dot_general(
            first[...], second, (((0,), (0,)), ((), ())), preferred_element_type=f32
        )
        value = (scale * value).astype(half)
        value = value.reshape(ref.shape[:-1] + (value.shape[-1],))
        if number == 2:
            ref[...] = jnp.zeros(ref.shape, half)
            ref[..., :tail] = value
        else:
            ref[...] = value

    local = [
        pltpu.make_async_copy(inmom.at[chip, core], k["momin"], k["lsem"].at[0]),
        pltpu.make_async_copy(outmom.at[:, chip, core], k["momout"], k["lsem"].at[1]),
    ]
    for copy in local:
        copy.start()
    greet_peers(core, chip, shard, chips, shards)
    stages = [
        sorted((d for d in range(1, chips) if low_phase(d, phases) == p), reverse=True)
        for p in range(phases)
    ] + [[0]]
    go(remote(small, k["tcore"], k["ts"].at[0], k["tr"].at[0], partner))
    for stage in ([0], range(1, phases + 1)):
        for number in order:
            if 0 in stage:
                own_grad(number)
            for p in stage:
                for d in stages[p]:
                    go(
                        remote(
                            source(number, block_at(chip, flips_of(number), d), 1 - core),
                            k[f"first{number}"].at[d],
                            k["ds"].at[number, d], k["dr"].at[number, d], partner,
                        )
                    )
    for copy in local:
        copy.wait()
    k["momt"][...] = jnp.zeros(k["momt"].shape, f32)
    k["momt"][:, : tail] = k["momin"][:, 2 * wide :]

    def moment(number):
        if number == 3:
            return k["momout"]
        if number == 2:
            return k["momt"]
        return k["momin"].at[:, pl.ds(offsets[number], wide)]

    def send_moment(number):
        return remote(
            moment(number), k["momr" + kinds[number]].at[shard],
            k["ms"].at[number], k["mr"].at[shard], {"shard": owners[number]},
        )

    for number in range(count):

        @pl.when(shard != owners[number])
        def _():
            send_moment(number).start()

        @pl.when(shard == owners[number])
        def _():
            k["momr" + kinds[number]][shard] = moment(number)[...]

    def send_plane(number):
        return remote(
            k[f"sums{number}"].at[0], k["third" + kinds[number]].at[shard],
            k["zs"].at[number], k["zr"].at[shard], {"shard": owners[number]},
        )

    def reduce_step(number, d):
        last = low_phase(d, phases)
        flips = flips_of(number)
        slot = k[f"first{number}"].at[d]
        remote(slot, slot, k["ds"].at[number, d], k["dr"].at[number, d], partner).wait_recv()
        total = source(number, block_at(chip, flips, d), core)[...].astype(f32)
        total = total + slot[...].astype(f32)
        for q in range(last):
            came = d + (1 << q)
            slot = k[f"recv{number}"].at[came]
            peer = {"rep": 2 * (chip + flips[q]) + core}
            remote(slot, slot, k["rs"].at[number, came], k["rr"].at[number, came], peer).wait_recv()
            total = total + slot[...].astype(f32)
        k[f"sums{number}"][d] = total.astype(half)
        if d:
            peer = {"rep": 2 * (chip + flips[last]) + core}
            go(
                remote(
                    k[f"sums{number}"].at[d], k[f"recv{number}"].at[d],
                    k["rs"].at[number, d], k["rr"].at[number, d], peer,
                )
            )
        else:

            @pl.when(shard != owners[number])
            def _():
                send_plane(number).start()

            @pl.when(shard == owners[number])
            def _():
                k["third" + kinds[number]][shard] = k[f"sums{number}"][0]

    def small_step(j):
        if j == 0:
            remote(small, k["tcore"], k["ts"].at[0], k["tr"].at[0], partner).wait_recv()
            k["tacc"][0] = small[...] + k["tcore"][...]
        else:
            slot = k["trecv"].at[j - 1]
            peer = {"rep": 2 * (chip + base_flips[j - 1]) + core}
            remote(slot, slot, k["ts"].at[j], k["tr"].at[j], peer).wait_recv()
            k["tacc"][j] = k["tacc"][j - 1] + slot[...]
        if j < phases:
            peer = {"rep": 2 * (chip + base_flips[j]) + core}
            go(
                remote(
                    k["tacc"].at[j], k["trecv"].at[j], k["ts"].at[j + 1], k["tr"].at[j + 1], peer
                )
            )
        else:
            k["tz"][shard] = k["tacc"][phases]
            for other in line:
                go(
                    remote(
                        k["tacc"].at[phases], k["tz"].at[shard],
                        k["tzs"].at[other], k["tzr"].at[shard], {"shard": other},
                    )
                )

    for number in order:
        for d in stages[0]:
            reduce_step(number, d)
    small_step(0)
    steps = 1
    for turn in range(count + phases - 1):
        for p in range(1, phases + 1):
            spot = turn - (p - 1)
            if 0 <= spot < count:
                for d in stages[p]:
                    reduce_step(order[spot], d)
        if steps <= phases:
            small_step(steps)
            steps += 1

    def grad_slot(number):
        ref = k["g" + kinds[number]]
        if number == 3:
            return lambda block, which: ref.at[:, block, which]
        if number == 2:
            return lambda block, which: ref.at[block, which]
        return lambda block, which: ref.at[number, block, which]

    def orth_slot(number):
        ref = k["o" + kinds[number]]
        if number == 3:
            return lambda block, which: ref.at[:, block, which]
        if number == 2:
            return lambda block, which: ref.at[block, which]
        return lambda block, which: ref.at[number, block, which]

    grad_spreads = [
        Spread(grad_slot(number), [k["g" + s] for s in ("xs", "xr", "ps", "pr")], (number,), turned[number])
        for number in range(count)
    ]
    orth_spreads = [
        Spread(orth_slot(number), [k["o" + s] for s in ("xs", "xr", "ps", "pr")], (number,), turned[number])
        for number in range(count)
    ]

    def grads_first():
        for number in order:

            @pl.when(shard != owners[number])
            def _():
                slot = grad_slot(number)(chip, core)
                remote(
                    slot, slot, k["gzs"].at[0], k["gzr"].at[number], {"shard": owners[number]}
                ).wait_recv()

            grad_spreads[number].start(0)

    def grads_second():
        for pattern in range(1, chips):
            for number in order:
                grad_spreads[number].wait(pattern)
                grad_spreads[number].start(pattern)

    def hooks(turn):
        pl.when(turn == 1)(grads_first)
        pl.when(turn == 3)(grads_second)

    def finish_poly(gram, gram_ref, poly_ref):
        gram_ref[...] = gram.astype(half)
        gram = gram_ref[...]
        square = jnp.dot(gram, gram, preferred_element_type=f32)
        poly_ref[...] = (
            schulz_coeffs[1] * gram.astype(f32) + schulz_coeffs[2] * square
        ).astype(half)

    def iterate_left(cur, gram_ref, poly_ref):
        tall, across = cur.shape
        size = min(tall, across)

        @pl.loop(0, NS_STEPS)
        def _(turn):
            hooks(turn)
            now = cur[...]
            finish_poly(
                lax.dot_general(now, now, (((1,), (1,)), ((), ())), preferred_element_type=f32),
                gram_ref, poly_ref,
            )
            for q in range(across // size):
                part = cur[:, q * size : (q + 1) * size]
                cur[:, q * size : (q + 1) * size] = (
                    schulz_coeffs[0] * part.astype(f32)
                    + jnp.dot(poly_ref[...], part, preferred_element_type=f32)
                ).astype(half)

    def iterate_right(cur, gram_ref, poly_ref):
        tall, across = cur.shape
        size = math.gcd(tall, 512)

        @pl.loop(0, NS_STEPS)
        def _(turn):
            hooks(turn)
            gram = jnp.zeros((across, across), f32)
            for q in range(tall // size):
                part = cur[q * size : (q + 1) * size]
                gram = gram + lax.dot_general(
                    part, part, (((0,), (0,)), ((), ())), preferred_element_type=f32
                )
            finish_poly(gram, gram_ref, poly_ref)
            for q in range(tall // size):
                part = cur[q * size : (q + 1) * size]
                cur[q * size : (q + 1) * size] = (
                    schulz_coeffs[0] * part.astype(f32)
                    + jnp.dot(part, poly_ref[...], preferred_element_type=f32)
                ).astype(half)

    def own_work(kind, number):
        third, momr, buf, cur = [k[name + kind] for name in ("third", "momr", "buf", "cur")]
        gsend = k["gsend" + kind]
        folded = kind == "o"

        def piece(side):
            part = buf.at[pl.ds(side * (shards // 2), shards // 2)]
            if folded:
                return lambda block, which: part.at[:, :, block, which]
            return lambda block, which: part.at[:, block, which]

        def rows(ref, block, which):
            if kind == "l":
                return ref.at[number, block, which]
            return ref.at[:, block, which] if folded else ref.at[block, which]

        for other in line:
            slot = third.at[other]
            remote(slot, slot, k["zs"].at[0], k["zr"].at[other], {"shard": other}).wait_recv()
            slot = momr.at[other]
            remote(slot, slot, k["ms"].at[0], k["mr"].at[other], {"shard": other}).wait_recv()
        total = third[0].astype(f32)
        for z in range(1, shards):
            total = total + third[z].astype(f32)
        merged = (momentum_keep * momr[...] + total).astype(half)
        if folded:
            buf[:, :, chip, core] = merged
        else:
            buf[:, chip, core] = merged
        spreads = [
            Spread(piece(side), [k["b" + s] for s in ("xs", "xr", "ps", "pr")], (side,), side == 1)
            for side in range(2)
        ]
        for spread in spreads:
            spread.start(0)
        gsend[...] = total.astype(half)

        def send_grad(other):
            return remote(
                gsend.at[other], rows(k["g" + kind], chip, core),
                k["gzs"].at[other], k["gzr"].at[number], {"shard": other},
            )

        for other in line:
            send_grad(other).start()
        rows(k["g" + kind], chip, core)[...] = gsend[shard]
        for pattern in range(1, chips):
            for spread in spreads:
                spread.wait(pattern)
                spread.start(pattern)
        for spread in spreads:
            spread.wait_partner()
        matrix = buf[...].reshape(cur.shape).astype(f32)
        frobenius = jnp.sqrt(jnp.sum(matrix * matrix))
        cur[...] = (matrix / (frobenius + 1e-07)).astype(half)
        if kind == "l":
            iterate_left(cur, k["graml"], k["polyl"])
        else:
            iterate_right(cur, k["gram" + kind], k["poly" + kind])
        for spread in spreads:
            spread.wait_sends()
        buf[...] = cur[...].reshape(buf.shape)

        def back(other):
            part = buf.at[other]
            part = part.at[:, chip, core] if folded else part.at[chip, core]
            return remote(
                part, rows(k["o" + kind], chip, core),
                k["ozs"].at[other], k["ozr"].at[number], {"shard": other},
            )

        for other in line:
            back(other).start()
        if kind == "l":
            k["ol"][number] = buf[shard]
        else:
            k["o" + kind][...] = buf[shard]
        for other in line:
            send_grad(other).wait_send()
            back(other).wait_send()

    def is_owner(numbers):
        flag = shard == owners[numbers[0]]
        for number in numbers[1:]:
            flag = jnp.logical_or(flag, shard == owners[number])
        return flag

    pl.when(is_owner((0, 1)))(lambda: own_work("l", lax.div(shard * count, shards)))
    pl.when(is_owner((2,)))(lambda: own_work("t", 2))
    pl.when(is_owner((3,)))(lambda: own_work("o", 3))
    if shards > count:

        @pl.when(jnp.logical_not(is_owner(range(count))))
        def _():
            grads_first()
            grads_second()

    back_order = (2, 0, 1, 3)
    for number in back_order:

        @pl.when(shard != owners[number])
        def _():
            slot = orth_slot(number)(chip, core)
            remote(
                slot, slot, k["ozs"].at[0], k["ozr"].at[number], {"shard": owners[number]}
            ).wait_recv()
            orth_spreads[number].start(0)

    for other in line:
        slot = k["tz"].at[other]
        remote(slot, slot, k["tzs"].at[other], k["tzr"].at[other], {"shard": other}).wait_recv()
    total = k["tz"][0]
    for z in range(1, shards):
        total = total + k["tz"][z]
    k["ftiny"][...] = total
    for spread in grad_spreads:
        spread.wait_partner()
    for number in back_order:

        @pl.when(shard != owners[number])
        def _():
            for pattern in range(1, chips):
                orth_spreads[number].wait(pattern)
                orth_spreads[number].start(pattern)

    for copy in started:
        copy.wait_send()
    for number in range(count):

        @pl.when(shard != owners[number])
        def _():
            send_moment(number).wait_send()
            send_plane(number).wait_send()

        grad_spreads[number].wait_sends()
    for number in back_order:

        @pl.when(shard != owners[number])
        def _():
            orth_spreads[number].wait_partner()
            orth_spreads[number].wait_sends()


def reduce_and_orthogonalize(normed, dproj, mixed, livecot, scale, small, inmom, out_moment, wide):
    chips = lax.axis_size("rep") // 2
    shards = lax.axis_size("shard")
    half = jnp.bfloat16
    f32 = jnp.float32
    height, columns = normed.shape[1], dproj.shape[1]
    depth = livecot.shape[1]
    rows = height // (shards * chips * 2)
    folds = mixed.shape[1] // height
    tail = columns - 2 * wide
    thin = -(-tail // LANES) * LANES
    outmom = out_moment.reshape(folds, chips, 2, rows, depth)
    outs = {
        "gl": ((2, chips, 2, rows, wide), half),
        "gt": ((chips, 2, rows, thin), half),
        "go": ((folds, chips, 2, rows, depth), half),
        "ol": ((2, chips, 2, rows, wide), half),
        "ot": ((chips, 2, rows, thin), half),
        "oo": ((folds, chips, 2, rows, depth), half),
        "ftiny": (small.shape, f32),
    }
    tails = [(rows, wide), (rows, wide), (rows, thin), (folds, rows, depth)]
    scratch = {
        "momin": ((rows, columns), f32),
        "momout": ((folds, rows, depth), f32),
        "momt": ((rows, thin), f32),
        "tcore": (small.shape, f32),
        "tacc": ((chips.bit_length(),) + small.shape, f32),
        "trecv": ((chips.bit_length(),) + small.shape, f32),
        "tz": ((shards,) + small.shape, f32),
    }
    for number, part in enumerate(tails):
        whole = ((shards, folds) if number == 3 else (shards,)) + (chips, 2, rows, part[-1])
        scratch[f"grad{number}"] = (whole, half)
        for name in ("first", "sums", "recv"):
            scratch[f"{name}{number}"] = ((chips, shards) + part, half)
    full = {
        "l": ((shards, chips, 2, rows, wide), (height, wide), height),
        "t": ((shards, chips, 2, rows, thin), (height, thin), thin),
        "o": ((shards, folds, chips, 2, rows, depth), (height * folds, depth), depth),
    }
    for kind, number in (("l", 0), ("t", 2), ("o", 3)):
        scratch["third" + kind] = ((shards, shards) + tails[number], half)
        scratch["momr" + kind] = ((shards,) + tails[number], f32)
        scratch["gsend" + kind] = ((shards,) + tails[number], half)
        scratch["buf" + kind] = (full[kind][0], half)
        scratch["cur" + kind] = (full[kind][1], half)
        scratch["gram" + kind] = ((full[kind][2],) * 2, half)
        scratch["poly" + kind] = ((full[kind][2],) * 2, half)
    sems = {
        "lsem": (2,),
        "ts": (chips.bit_length(),),
        "tr": (chips.bit_length(),),
        "tzs": (shards,),
        "tzr": (shards,),
        "zs": (4,),
        "zr": (shards,),
        "ms": (4,),
        "mr": (shards,),
        "gzs": (shards,),
        "gzr": (4,),
        "ozs": (shards,),
        "ozr": (4,),
    }
    for name in ("ds", "dr", "rs", "rr"):
        sems[name] = (4, chips)
    for name in ("xs", "xr", "ps", "pr"):
        sems["b" + name] = (2, chips)
        sems["g" + name] = (4, chips)
        sems["o" + name] = (4, chips)
    vmem = pl.BlockSpec(memory_space=pltpu.VMEM)
    anywhere = pl.BlockSpec(memory_space=pl.ANY)
    names = list(outs) + list(scratch) + list(sems)
    return pl.pallas_call(
        functools.partial(update_kernel, names, tail, scale),
        out_shape=[jax.ShapeDtypeStruct(s, d) for s, d in outs.values()],
        in_specs=[vmem] * 5 + [anywhere] * 2,
        out_specs=[vmem] * len(outs),
        scratch_shapes=[pltpu.VMEM(s, d) for s, d in scratch.values()]
        + [pltpu.SemaphoreType.DMA(s) for s in sems.values()],
        compiler_params=pltpu.CompilerParams(
            collective_id=1, has_side_effects=True, vmem_limit_bytes=60 * 1024 * 1024
        ),
    )(normed, dproj, mixed, livecot, small, inmom, outmom)


def finish_kernel(
    sizes, gl, gt, go, ol, ot, oo, tiny, in_w, out_w, in_m, out_m,
    p_norm, p_gate, p_conv, p_head, a_norm, a_gate, a_conv, a_head,
    grad_in, grad_out, grad_norm, grad_gate, grad_conv, grad_head,
    new_in, new_out, mom_in, mom_out,
    n_norm, n_gate, n_conv, n_head, s_norm, s_gate, s_conv, s_head,
):
    f32 = jnp.float32
    wide = gl.shape[-1]
    tail = in_w.shape[0] - 2 * wide
    spans = ((0, wide), (wide, wide), (2 * wide, tail))
    for number, (low, width) in enumerate(spans):
        if number < 2:
            grad, orth = gl[number].astype(f32).T, ol[number].astype(f32).T
        else:
            grad, orth = gt[...].astype(f32).T[:width], ot[...].astype(f32).T[:width]
        here = slice(low, low + width)
        grad_in[here] = grad
        mom_in[here] = momentum_keep * in_m[here] + grad
        new_in[here] = muon_apply(in_w[here], orth, sizes[number])
    grad = go[...].astype(f32)
    grad_out[...] = grad
    mom_out[...] = momentum_keep * out_m[...] + grad
    new_out[...] = muon_apply(out_w[...], oo[...].astype(f32), sizes[3])

    def adam(grad, param, state):
        first = beta_first * state[0] + (1.0 - beta_first) * grad
        second = beta_second * state[1] + (1.0 - beta_second) * grad * grad
        first_hat = first / (1.0 - beta_first**ADAM_STEP)
        second_hat = second / (1.0 - beta_second**ADAM_STEP)
        updated = param - adam_rate * (
            first_hat / (jnp.sqrt(second_hat) + adam_eps) + decay_rate * param
        )
        return updated, first, second

    taps = p_conv.shape[0]
    conv = tiny[:taps]
    grad_conv[...] = conv
    n_conv[...], s_conv[:, 0], s_conv[:, 1] = adam(conv, p_conv[...], (a_conv[:, 0], a_conv[:, 1]))
    for row, grad_ref, p, a, n, s in (
        (taps, grad_gate, p_gate, a_gate, n_gate, s_gate),
        (taps + 1, grad_norm, p_norm, a_norm, n_norm, s_norm),
    ):
        grad = tiny[row : row + 1, : p.shape[1]]
        grad_ref[...] = grad
        n[...], s[0:1], s[1:2] = adam(grad, p[...], (a[0:1], a[1:2]))
    heads = p_head.shape[1]
    for i in range(p_head.shape[0]):
        grad = tiny[taps + 2 : taps + 3, i * LANES : i * LANES + heads]
        one = slice(i, i + 1)
        grad_head[one] = grad
        n_head[one], s_head[i, 0:1], s_head[i, 1:2] = adam(
            grad, p_head[one], (a_head[i, 0:1], a_head[i, 1:2])
        )


def pack_small(grad_norm, grad_gate, grad_conv, grad_head):
    width = grad_conv.shape[1]

    def fit(row):
        return jnp.pad(row, ((0, 0), (0, width - row.shape[1])))

    heads = [jnp.pad(grad_head[i][None], ((0, 0), (0, LANES - grad_head.shape[1]))) for i in range(3)]
    packed = jnp.concatenate(
        [grad_conv, fit(grad_gate[None]), fit(grad_norm[None]), fit(jnp.concatenate(heads, 1))], 0
    )
    return jnp.pad(packed, ((0, -packed.shape[0] % 8), (0, 0)))


def local(
    tokens,
    cotangent,
    block_fill,
    block_start,
    in_weight,
    out_weight,
    in_moment,
    out_moment,
    norm_gain,
    gate_gain,
    conv_params,
    head_params,
    adam_norm,
    adam_gate,
    adam_conv,
    adam_head,
):
    shards = lax.axis_size("shard")
    replicas = lax.axis_size("rep")
    whole_in, whole_out, moment = gather_rows(in_weight, out_weight, in_moment)
    results = device_pass(
        tokens,
        cotangent,
        block_fill,
        block_start,
        whole_in,
        whole_out,
        whole_in,
        whole_out,
        norm_gain,
        gate_gain,
        conv_params,
        head_params,
    )
    activations, input_grad, factors, grad_norm, grad_gate, grad_conv, grad_head = results
    scale = 1.0 / math.sqrt(tokens.shape[0] * shards * replicas)
    wide = gate_gain.shape[0]
    gl, gt, go, ol, ot, oo, tiny = reduce_and_orthogonalize(
        *factors,
        scale,
        scale * pack_small(grad_norm, grad_gate, grad_conv, grad_head),
        moment,
        out_moment,
        wide,
    )
    rows = in_weight.shape[0]
    tail = in_weight.shape[1] - 2 * wide
    sizes = (
        (rows * shards, wide),
        (rows * shards, wide),
        (rows * shards, tail),
        (out_weight.shape[0] * shards, out_weight.shape[1]),
    )
    pieces = []
    for l, t, o in ((gl, gt, go), (ol, ot, oo)):
        pieces += [l.reshape(2, rows, wide), t.reshape(rows, -1), o.reshape(out_weight.shape)]
    params = [norm_gain[None], gate_gain[None], conv_params, head_params]
    states = [adam_norm, adam_gate, jnp.swapaxes(adam_conv, 0, 1), jnp.swapaxes(adam_head, 0, 1)]
    weights = [in_weight.T, out_weight]
    moments = [in_moment.T, out_moment]
    like = weights + params + weights * 2 + params + states
    vmem = pl.BlockSpec(memory_space=pltpu.VMEM)
    done = pl.pallas_call(
        functools.partial(finish_kernel, sizes),
        out_shape=[jax.ShapeDtypeStruct(a.shape, a.dtype) for a in like],
        in_specs=[vmem] * (11 + 8),
        out_specs=[vmem] * len(like),
        compiler_params=pltpu.CompilerParams(vmem_limit_bytes=60 * 1024 * 1024),
    )(*pieces, tiny, *weights, *moments, *params, *states)
    done = list(done)
    for spot, gain in ((2, norm_gain), (3, gate_gain), (10, norm_gain), (11, gate_gain)):
        done[spot] = done[spot].reshape(gain.shape)
    for spot in (0, 6, 8):
        done[spot] = done[spot].T
    for spot in (16, 17):
        done[spot] = jnp.swapaxes(done[spot], 0, 1)
    return (activations, input_grad, *done)


def solution(mesh):
    return jax.shard_map(
        local,
        mesh=mesh,
        in_specs=(
            P(("rep", "shard"), None),
            P(("rep", "shard"), None),
            P(("rep", "shard")),
            P(("rep", "shard")),
            P("shard", None),
            P("shard", None),
            P("shard", None),
            P("shard", None),
            P(),
            P(),
            P(),
            P(),
            P(),
            P(),
            P(),
            P(),
        ),
        out_specs=(
            P(("rep", "shard"), None),
            P(("rep", "shard"), None),
            P("shard", None),
            P("shard", None),
            P(),
            P(),
            P(),
            P(),
            P("shard", None),
            P("shard", None),
            P("shard", None),
            P("shard", None),
            P(),
            P(),
            P(),
            P(),
            P(),
            P(),
            P(),
            P(),
        ),
        check_vma=False,
    )
```

```python
import functools
import math

import jax
import jax.numpy as jnp
from jax import lax
from jax.experimental import pallas as pl
from jax.experimental.pallas import tpu as pltpu
from jax.sharding import PartitionSpec as P

NS_STEPS = 5
ADAM_STEP = 3


ssd_precision = lax.Precision.HIGH
norm_eps = 1e-05
schulz_coeffs = (3.4445, -4.775, 2.0315)
momentum_keep = 0.95
muon_rate = 0.05
adam_rate = 0.2
beta_first = 0.9
beta_second = 0.95
decay_rate = 0.1
adam_eps = 1e-08


def pre_norm(base, gain):
    return base * lax.rsqrt(jnp.mean(base * base, -1, keepdims=True) + norm_eps) * gain


def mixer(proj, conv_params, head_params, gate_gain, starts):
    total = proj.shape[0]
    blocks = starts.shape[0]
    length = total // blocks
    width_inner = gate_gain.shape[0]
    heads = head_params.shape[1]
    head_size = width_inner // heads
    taps = conv_params.shape[0] - 1
    channels = conv_params.shape[1]
    state_size = (channels - width_inner) // 2
    gate_in = proj[:, :width_inner]
    conv_in = proj[:, width_inner : width_inner + channels]
    dt_raw = proj[:, width_inner + channels :]
    seq_block = jnp.cumsum(starts)
    seq_token = jnp.repeat(seq_block, length)
    summed = conv_params[taps] + conv_params[taps - 1] * conv_in
    for offset in range(1, taps):
        moved = jnp.concatenate([jnp.zeros((offset, channels), jnp.float32), conv_in[:-offset]], 0)
        moved_seq = jnp.concatenate([jnp.full((offset,), -1, jnp.int32), seq_token[:-offset]], 0)
        same_seq = (moved_seq == seq_token).astype(jnp.float32)
        summed = summed + conv_params[taps - 1 - offset] * moved * same_seq[:, None]
    activated = jax.nn.silu(summed)
    values = activated[:, :width_inner].reshape(total, heads, head_size)
    b_input = activated[:, width_inner : width_inner + state_size]
    c_input = activated[:, width_inner + state_size :]
    step_size = jax.nn.softplus(dt_raw + head_params[0])
    rates = -jnp.exp(head_params[1])
    lower = jnp.tril(jnp.ones((total, total), jnp.bool_))
    mask = jnp.logical_and(lower, seq_token[:, None] == seq_token[None, :])
    columns = jnp.einsum(
        "ts,sh->ht", lower.astype(jnp.float32), step_size * rates, precision=lax.Precision.HIGHEST
    )
    spread = columns[:, :, None] - columns[:, None, :]
    decay = jnp.where(mask, jnp.exp(jnp.where(mask, spread, 0.0)), 0.0)
    scores = jnp.dot(c_input, b_input.T, precision=ssd_precision)
    weighted = values * step_size[:, :, None]
    outputs = jnp.einsum(
        "hts,shp->thp", decay * scores[None], weighted, precision=ssd_precision
    )
    outputs = outputs + head_params[2][None, :, None] * values
    gated = outputs.reshape(total, width_inner) * jax.nn.silu(gate_in)
    return gated * lax.rsqrt(jnp.mean(gated * gated, -1, keepdims=True) + norm_eps) * gate_gain


def device_pass(
    tokens,
    cotangent,
    fill,
    starts,
    fwd_in,
    fwd_out,
    back_in,
    back_out,
    norm_gain,
    gate_gain,
    conv_params,
    head_params,
):
    total = tokens.shape[0]
    length = total // fill.shape[0]
    position = jnp.arange(total, dtype=jnp.int32) % length
    live = position < jnp.repeat(fill, length)
    base = tokens.astype(jnp.float32)
    normed, norm_back = jax.vjp(pre_norm, base, norm_gain)
    normed16 = normed.astype(jnp.bfloat16)
    proj = jnp.dot(normed16, fwd_in, preferred_element_type=jnp.float32)

    def mix_piece(proj_in, conv_in, head_in, gain_in):
        return mixer(proj_in, conv_in, head_in, gain_in, starts)

    mixed, mixer_back = jax.vjp(mix_piece, proj, conv_params, head_params, gate_gain)
    mixed16 = mixed.astype(jnp.bfloat16)
    branch = jnp.dot(mixed16, fwd_out, preferred_element_type=jnp.float32)
    activations = jnp.where(live[:, None], base + branch, 0.0).astype(jnp.bfloat16)
    live_cot = jnp.where(live[:, None], cotangent, jnp.zeros_like(cotangent))
    d_mixed = jnp.dot(live_cot, back_out.T, preferred_element_type=jnp.float32)
    d_proj, grad_conv, grad_head, grad_gate = mixer_back(d_mixed)
    d_proj16 = d_proj.astype(jnp.bfloat16)
    d_normed = jnp.dot(d_proj16, back_in.T, preferred_element_type=jnp.float32)
    d_base, grad_norm = norm_back(d_normed)
    input_grad = live_cot.astype(jnp.float32) + d_base
    factors = (normed16, d_proj16.T, mixed16.T, live_cot)
    return (activations, input_grad, factors, grad_norm, grad_gate, grad_conv, grad_head)


def muon_apply(weight, orth, full_shape):
    factor = 0.2 * math.sqrt(max(full_shape[0], full_shape[1]))
    return weight - muon_rate * (factor * orth.astype(jnp.float32) + decay_rate * weight)


MESH = pl.DeviceIdType.MESH
LANES = 128


def places():
    rep = lax.axis_index("rep")
    shard = lax.axis_index("shard")
    core = lax.rem(rep, 2)
    chip = lax.div(rep, 2)
    chips = lax.axis_size("rep") // 2
    shards = lax.axis_size("shard")
    return rep, shard, core, chip, chips, shards


def line_order(shard, shards):
    tables = [
        sorted((z for z in range(shards) if z != here), key=lambda z: (abs(z - here), z))
        for here in range(shards)
    ]
    order = []
    for spot in range(shards - 1):
        value = jnp.int32(tables[0][spot])
        for here in range(1, shards):
            value = jnp.where(shard == here, jnp.int32(tables[here][spot]), value)
        order.append(value)
    return order


def plain_flips(chip, chips):
    count = chips.bit_length() - 1
    return [(1 << j) * (1 - 2 * lax.rem(lax.div(chip, 1 << j), 2)) for j in range(count)]


def turned_flips(chip, chips, turned):
    flips = plain_flips(chip, chips)
    return flips[::-1] if turned else flips


def block_at(chip, flips, pattern):
    for j, step in enumerate(flips):
        if pattern >> j & 1:
            chip = chip + step
    return chip


def greet_peers(core, chip, shard, chips, shards):
    barrier = pltpu.get_barrier_semaphore()
    peers = [{"rep": 2 * chip + 1 - core}]
    for step in plain_flips(chip, chips):
        peers.append({"rep": 2 * (chip + step) + core})
    for step in range(1, shards):
        peers.append({"shard": lax.rem(shard + step, shards)})
    for peer in peers:
        pl.semaphore_signal(barrier, inc=1, device_id=peer, device_id_type=MESH)
    pl.semaphore_wait(barrier, len(peers))


def remote(src, dst, send, recv, peer):
    return pltpu.make_async_remote_copy(
        src_ref=src, dst_ref=dst, send_sem=send, recv_sem=recv, device_id=peer, device_id_type=MESH
    )


class Spread:
    def __init__(self, slot, sems, index, turned):
        rep, shard, core, chip, chips, shards = places()
        self.slot = slot
        self.xs, self.xr, self.ps, self.pr = [
            (lambda q, s=s: s.at[tuple(index) + (q,)]) for s in sems
        ]
        self.chips, self.chip, self.core = chips, chip, core
        self.flips = turned_flips(chip, chips, turned)
        self.partner = {"rep": 2 * chip + 1 - core}

    def hops(self, pattern):
        ref = self.slot(block_at(self.chip, self.flips, pattern), self.core)
        copies = []
        for phase in range(pattern.bit_length(), len(self.flips)):
            q = pattern + (1 << phase)
            peer = {"rep": 2 * (self.chip + self.flips[phase]) + self.core}
            copies.append(remote(ref, ref, self.xs(q), self.xr(q), peer))
        copies.append(remote(ref, ref, self.ps(pattern), self.pr(pattern), self.partner))
        return copies

    def start(self, pattern):
        for copy in self.hops(pattern):
            copy.start()

    def wait(self, pattern):
        ref = self.slot(block_at(self.chip, self.flips, pattern), self.core)
        phase = pattern.bit_length() - 1
        peer = {"rep": 2 * (self.chip + self.flips[phase]) + self.core}
        remote(ref, ref, self.xs(pattern), self.xr(pattern), peer).wait_recv()

    def wait_partner(self):
        for pattern in range(self.chips):
            ref = self.slot(block_at(self.chip, self.flips, pattern), 1 - self.core)
            remote(ref, ref, self.ps(pattern), self.pr(pattern), self.partner).wait_recv()

    def wait_sends(self):
        for pattern in range(self.chips):
            for copy in self.hops(pattern):
                copy.wait_send()


def gather_kernel(
    in_ref, out_ref, mom_ref, all_in, all_out, mom_rows,
    flat_in, send_in, send_out, zs, zr, xs, xr, ps, pr,
):
    rep, shard, core, chip, chips, shards = places()
    half = jnp.bfloat16
    rows = flat_in.shape[1]
    turned = in_ref[...].T
    for j in range(2 * chips):
        flat_in[j] = turned[j * rows : (j + 1) * rows]
    send_in[...] = flat_in[2 * chip + core].astype(half)
    send_out[...] = out_ref[chip, core].astype(half)
    greet_peers(core, chip, shard, chips, shards)
    pairs = ((send_in, all_in), (send_out, all_out))

    def hop(a, origin, src, sign):
        return remote(
            src, pairs[a][1].at[origin, chip, core],
            zs.at[a, origin, (sign + 1) // 2], zr.at[a, origin], {"shard": shard + sign},
        )

    def room(sign):
        return shard + 1 < shards if sign > 0 else shard > 0

    for a, (send, dst) in enumerate(pairs):
        for sign in (1, -1):

            @pl.when(room(sign))
            def _():
                hop(a, shard, send, sign).start()

    for j in range(2 * chips):
        all_in[shard, j // 2, j % 2] = flat_in[j].astype(half)
    all_out[shard] = out_ref[...].astype(half)
    moment = mom_ref[...].T
    for j in range(2 * chips):
        mom_rows[j] = moment[j * rows : (j + 1) * rows]

    def far(step, sign):
        origin = shard - sign * step
        held = origin >= 0 if sign > 0 else origin < shards
        return origin, held

    visits = [
        (a, step, sign)
        for a in range(2)
        for step in range(1, shards)
        for sign in (1, -1)
    ]

    def spread_of(a, step, sign):
        origin, held = far(step, sign)
        dst = pairs[a][1]
        sems = [ref for ref in (xs, xr, ps, pr)]
        odd = (step + (sign > 0) + a) % 2 == 1
        return Spread(lambda block, k: dst.at[origin, block, k], sems, (a, origin), odd), held

    for a, step, sign in visits:
        origin, held = far(step, sign)

        @pl.when(held)
        def _():
            slot = pairs[a][1].at[origin, chip, core]
            hop(a, origin, slot, sign).wait_recv()

            @pl.when(room(sign))
            def _():
                hop(a, origin, slot, sign).start()

            spread_of(a, step, sign)[0].start(0)

    for pattern in range(1, chips):
        for a, step, sign in visits:
            spread, held = spread_of(a, step, sign)

            @pl.when(held)
            def _():
                spread.wait(pattern)
                spread.start(pattern)

    for a, step, sign in visits:
        origin, held = far(step, sign)

        @pl.when(held)
        def _():
            spread = spread_of(a, step, sign)[0]
            spread.wait_partner()
            spread.wait_sends()

            @pl.when(room(sign))
            def _():
                hop(a, origin, pairs[a][1].at[origin, chip, core], sign).wait_send()

    for a, (send, dst) in enumerate(pairs):
        for sign in (1, -1):

            @pl.when(room(sign))
            def _():
                hop(a, shard, send, sign).wait_send()


def gather_rows(in_weight, out_weight, in_moment):
    chips = lax.axis_size("rep") // 2
    shards = lax.axis_size("shard")
    half = jnp.bfloat16
    f32 = jnp.float32
    height, columns = in_weight.shape
    rows = height // (2 * chips)
    depth = out_weight.shape[1]
    out_rows = out_weight.shape[0] // (2 * chips)
    vmem = pl.BlockSpec(memory_space=pltpu.VMEM)
    dma = pltpu.SemaphoreType.DMA
    whole_in, whole_out, moment = pl.pallas_call(
        gather_kernel,
        out_shape=[
            jax.ShapeDtypeStruct((shards, chips, 2, rows, columns), half),
            jax.ShapeDtypeStruct((shards, chips, 2, out_rows, depth), half),
            jax.ShapeDtypeStruct((2 * chips, rows, columns), f32),
        ],
        in_specs=[vmem] * 3,
        out_specs=[vmem] * 3,
        scratch_shapes=[
            pltpu.VMEM((2 * chips, rows, columns), f32),
            pltpu.VMEM((rows, columns), half),
            pltpu.VMEM((out_rows, depth), half),
            dma((2, shards, 2)),
            dma((2, shards)),
        ]
        + [dma((2, shards, chips))] * 4,
        compiler_params=pltpu.CompilerParams(
            collective_id=0, has_side_effects=True, vmem_limit_bytes=60 * 1024 * 1024
        ),
    )(in_weight.T, out_weight.reshape(chips, 2, out_rows, depth), in_moment.T)
    return (
        whole_in.reshape(shards * height, columns),
        whole_out.reshape(shards * out_weight.shape[0], depth),
        moment.reshape(chips, 2, rows, columns),
    )


def low_phase(pattern, phases):
    return phases if pattern == 0 else (pattern & -pattern).bit_length() - 1


def update_kernel(names, tail, scale, normed, dproj, mixed, livecot, small, inmom, outmom, *refs):
    k = dict(zip(names, refs))
    rep, shard, core, chip, chips, shards = places()
    f32 = jnp.float32
    half = jnp.bfloat16
    partner = {"rep": 2 * chip + 1 - core}
    base_flips = plain_flips(chip, chips)
    phases = len(base_flips)
    turned = (False, True, True, False)
    wide = k["gl"].shape[-1]
    thin = k["gt"].shape[-1]
    count = 4
    kinds = ("l", "l", "t", "o")
    offsets = (0, wide, 2 * wide)
    widths = (wide, wide, thin)
    owners = [number * shards // count for number in range(count)]
    order = (3, 0, 1, 2)
    line = line_order(shard, shards)
    started = []

    def go(copy):
        copy.start()
        started.append(copy)

    def source(number, block, which):
        ref = k[f"grad{number}"]
        return ref.at[:, :, block, which] if number == 3 else ref.at[:, block, which]

    def flips_of(number):
        return turned_flips(chip, chips, turned[number])

    def own_grad(number):
        ref = k[f"grad{number}"]
        if number == 3:
            value = jnp.dot(mixed[...], livecot[...], preferred_element_type=f32)
        else:
            low = offsets[number]
            part = dproj[low : low + (tail if number == 2 else wide)]
            value = lax.dot_general(
                normed[...].T, part, (((1,), (1,)), ((), ())), preferred_element_type=f32
            )
        value = (scale * value).astype(half)
        value = value.reshape(ref.shape[:-1] + (value.shape[-1],))
        if number == 2:
            ref[...] = jnp.zeros(ref.shape, half)
            ref[..., :tail] = value
        else:
            ref[...] = value

    local = [
        pltpu.make_async_copy(inmom.at[chip, core], k["momin"], k["lsem"].at[0]),
        pltpu.make_async_copy(outmom.at[:, chip, core], k["momout"], k["lsem"].at[1]),
    ]
    for copy in local:
        copy.start()
    greet_peers(core, chip, shard, chips, shards)
    stages = [
        sorted((d for d in range(1, chips) if low_phase(d, phases) == p), reverse=True)
        for p in range(phases)
    ] + [[0]]
    go(remote(small, k["tcore"], k["ts"].at[0], k["tr"].at[0], partner))
    for stage in ([0], range(1, phases + 1)):
        for number in order:
            if 0 in stage:
                own_grad(number)
            for p in stage:
                for d in stages[p]:
                    go(
                        remote(
                            source(number, block_at(chip, flips_of(number), d), 1 - core),
                            k[f"first{number}"].at[d],
                            k["ds"].at[number, d], k["dr"].at[number, d], partner,
                        )
                    )
    for copy in local:
        copy.wait()
    k["momt"][...] = jnp.zeros(k["momt"].shape, f32)
    k["momt"][:, : tail] = k["momin"][:, 2 * wide :]

    def moment(number):
        if number == 3:
            return k["momout"]
        if number == 2:
            return k["momt"]
        return k["momin"].at[:, pl.ds(offsets[number], wide)]

    def send_moment(number):
        return remote(
            moment(number), k["momr" + kinds[number]].at[shard],
            k["ms"].at[number], k["mr"].at[shard], {"shard": owners[number]},
        )

    for number in range(count):

        @pl.when(shard != owners[number])
        def _():
            send_moment(number).start()

        @pl.when(shard == owners[number])
        def _():
            k["momr" + kinds[number]][shard] = moment(number)[...]

    def send_plane(number):
        return remote(
            k[f"sums{number}"].at[0], k["third" + kinds[number]].at[shard],
            k["zs"].at[number], k["zr"].at[shard], {"shard": owners[number]},
        )

    def reduce_step(number, d):
        last = low_phase(d, phases)
        flips = flips_of(number)
        slot = k[f"first{number}"].at[d]
        remote(slot, slot, k["ds"].at[number, d], k["dr"].at[number, d], partner).wait_recv()
        total = source(number, block_at(chip, flips, d), core)[...].astype(f32)
        total = total + slot[...].astype(f32)
        for q in range(last):
            came = d + (1 << q)
            slot = k[f"recv{number}"].at[came]
            peer = {"rep": 2 * (chip + flips[q]) + core}
            remote(slot, slot, k["rs"].at[number, came], k["rr"].at[number, came], peer).wait_recv()
            total = total + slot[...].astype(f32)
        k[f"sums{number}"][d] = total.astype(half)
        if d:
            peer = {"rep": 2 * (chip + flips[last]) + core}
            go(
                remote(
                    k[f"sums{number}"].at[d], k[f"recv{number}"].at[d],
                    k["rs"].at[number, d], k["rr"].at[number, d], peer,
                )
            )
        else:

            @pl.when(shard != owners[number])
            def _():
                send_plane(number).start()

            @pl.when(shard == owners[number])
            def _():
                k["third" + kinds[number]][shard] = k[f"sums{number}"][0]

    def small_step(j):
        if j == 0:
            remote(small, k["tcore"], k["ts"].at[0], k["tr"].at[0], partner).wait_recv()
            k["tacc"][0] = small[...] + k["tcore"][...]
        else:
            slot = k["trecv"].at[j - 1]
            peer = {"rep": 2 * (chip + base_flips[j - 1]) + core}
            remote(slot, slot, k["ts"].at[j], k["tr"].at[j], peer).wait_recv()
            k["tacc"][j] = k["tacc"][j - 1] + slot[...]
        if j < phases:
            peer = {"rep": 2 * (chip + base_flips[j]) + core}
            go(
                remote(
                    k["tacc"].at[j], k["trecv"].at[j], k["ts"].at[j + 1], k["tr"].at[j + 1], peer
                )
            )
        else:
            k["tz"][shard] = k["tacc"][phases]
            for other in line:
                go(
                    remote(
                        k["tacc"].at[phases], k["tz"].at[shard],
                        k["tzs"].at[other], k["tzr"].at[shard], {"shard": other},
                    )
                )

    for number in order:
        for d in stages[0]:
            reduce_step(number, d)
    small_step(0)
    steps = 1
    for turn in range(count + phases - 1):
        for p in range(1, phases + 1):
            spot = turn - (p - 1)
            if 0 <= spot < count:
                for d in stages[p]:
                    reduce_step(order[spot], d)
        if steps <= phases:
            small_step(steps)
            steps += 1

    def grad_slot(number):
        ref = k["g" + kinds[number]]
        if number == 3:
            return lambda block, which: ref.at[:, block, which]
        if number == 2:
            return lambda block, which: ref.at[block, which]
        return lambda block, which: ref.at[number, block, which]

    def orth_slot(number):
        ref = k["o" + kinds[number]]
        if number == 3:
            return lambda block, which: ref.at[:, block, which]
        if number == 2:
            return lambda block, which: ref.at[block, which]
        return lambda block, which: ref.at[number, block, which]

    grad_spreads = [
        Spread(grad_slot(number), [k["g" + s] for s in ("xs", "xr", "ps", "pr")], (number,), turned[number])
        for number in range(count)
    ]
    orth_spreads = [
        Spread(orth_slot(number), [k["o" + s] for s in ("xs", "xr", "ps", "pr")], (number,), turned[number])
        for number in range(count)
    ]

    def grads_first():
        for number in order:

            @pl.when(shard != owners[number])
            def _():
                slot = grad_slot(number)(chip, core)
                remote(
                    slot, slot, k["gzs"].at[0], k["gzr"].at[number], {"shard": owners[number]}
                ).wait_recv()

            grad_spreads[number].start(0)

    def grads_second():
        for pattern in range(1, chips):
            for number in order:
                grad_spreads[number].wait(pattern)
                grad_spreads[number].start(pattern)

    def hooks(turn):
        pl.when(turn == 1)(grads_first)
        pl.when(turn == 3)(grads_second)

    def finish_poly(gram, gram_ref, poly_ref):
        gram_ref[...] = gram.astype(half)
        gram = gram_ref[...]
        square = jnp.dot(gram, gram, preferred_element_type=f32)
        poly_ref[...] = (
            schulz_coeffs[1] * gram.astype(f32) + schulz_coeffs[2] * square
        ).astype(half)

    def iterate_left(cur, gram_ref, poly_ref):
        tall, across = cur.shape
        size = min(tall, across)

        @pl.loop(0, NS_STEPS)
        def _(turn):
            hooks(turn)
            now = cur[...]
            finish_poly(
                lax.dot_general(now, now, (((1,), (1,)), ((), ())), preferred_element_type=f32),
                gram_ref, poly_ref,
            )
            for q in range(across // size):
                part = cur[:, q * size : (q + 1) * size]
                cur[:, q * size : (q + 1) * size] = (
                    schulz_coeffs[0] * part.astype(f32)
                    + jnp.dot(poly_ref[...], part, preferred_element_type=f32)
                ).astype(half)

    def iterate_right(cur, gram_ref, poly_ref):
        tall, across = cur.shape
        size = math.gcd(tall, 512)

        @pl.loop(0, NS_STEPS)
        def _(turn):
            hooks(turn)
            gram = jnp.zeros((across, across), f32)
            for q in range(tall // size):
                part = cur[q * size : (q + 1) * size]
                gram = gram + lax.dot_general(
                    part, part, (((0,), (0,)), ((), ())), preferred_element_type=f32
                )
            finish_poly(gram, gram_ref, poly_ref)
            for q in range(tall // size):
                part = cur[q * size : (q + 1) * size]
                cur[q * size : (q + 1) * size] = (
                    schulz_coeffs[0] * part.astype(f32)
                    + jnp.dot(part, poly_ref[...], preferred_element_type=f32)
                ).astype(half)

    def own_work(kind, number):
        third, momr, buf, cur = [k[name + kind] for name in ("third", "momr", "buf", "cur")]
        gsend = k["gsend" + kind]
        folded = kind == "o"

        def piece(side):
            part = buf.at[pl.ds(side * (shards // 2), shards // 2)]
            if folded:
                return lambda block, which: part.at[:, :, block, which]
            return lambda block, which: part.at[:, block, which]

        def rows(ref, block, which):
            if kind == "l":
                return ref.at[number, block, which]
            return ref.at[:, block, which] if folded else ref.at[block, which]

        for other in line:
            slot = third.at[other]
            remote(slot, slot, k["zs"].at[0], k["zr"].at[other], {"shard": other}).wait_recv()
            slot = momr.at[other]
            remote(slot, slot, k["ms"].at[0], k["mr"].at[other], {"shard": other}).wait_recv()
        total = third[0].astype(f32)
        for z in range(1, shards):
            total = total + third[z].astype(f32)
        merged = (momentum_keep * momr[...] + total).astype(half)
        if folded:
            buf[:, :, chip, core] = merged
        else:
            buf[:, chip, core] = merged
        spreads = [
            Spread(piece(side), [k["b" + s] for s in ("xs", "xr", "ps", "pr")], (side,), side == 1)
            for side in range(2)
        ]
        for spread in spreads:
            spread.start(0)
        gsend[...] = total.astype(half)

        def send_grad(other):
            return remote(
                gsend.at[other], rows(k["g" + kind], chip, core),
                k["gzs"].at[other], k["gzr"].at[number], {"shard": other},
            )

        for other in line:
            send_grad(other).start()
        rows(k["g" + kind], chip, core)[...] = gsend[shard]
        for pattern in range(1, chips):
            for spread in spreads:
                spread.wait(pattern)
                spread.start(pattern)
        for spread in spreads:
            spread.wait_partner()
        matrix = buf[...].reshape(cur.shape).astype(f32)
        frobenius = jnp.sqrt(jnp.sum(matrix * matrix))
        cur[...] = (matrix / (frobenius + 1e-07)).astype(half)
        if kind == "l":
            iterate_left(cur, k["graml"], k["polyl"])
        else:
            iterate_right(cur, k["gram" + kind], k["poly" + kind])
        for spread in spreads:
            spread.wait_sends()
        buf[...] = cur[...].reshape(buf.shape)

        def back(other):
            part = buf.at[other]
            part = part.at[:, chip, core] if folded else part.at[chip, core]
            return remote(
                part, rows(k["o" + kind], chip, core),
                k["ozs"].at[other], k["ozr"].at[number], {"shard": other},
            )

        for other in line:
            back(other).start()
        if kind == "l":
            k["ol"][number] = buf[shard]
        else:
            k["o" + kind][...] = buf[shard]
        for other in line:
            send_grad(other).wait_send()
            back(other).wait_send()

    def is_owner(numbers):
        flag = shard == owners[numbers[0]]
        for number in numbers[1:]:
            flag = jnp.logical_or(flag, shard == owners[number])
        return flag

    pl.when(is_owner((0, 1)))(lambda: own_work("l", lax.div(shard * count, shards)))
    pl.when(is_owner((2,)))(lambda: own_work("t", 2))
    pl.when(is_owner((3,)))(lambda: own_work("o", 3))
    if shards > count:

        @pl.when(jnp.logical_not(is_owner(range(count))))
        def _():
            grads_first()
            grads_second()

    back_order = (2, 0, 1, 3)
    for number in back_order:

        @pl.when(shard != owners[number])
        def _():
            slot = orth_slot(number)(chip, core)
            remote(
                slot, slot, k["ozs"].at[0], k["ozr"].at[number], {"shard": owners[number]}
            ).wait_recv()
            orth_spreads[number].start(0)

    for other in line:
        slot = k["tz"].at[other]
        remote(slot, slot, k["tzs"].at[other], k["tzr"].at[other], {"shard": other}).wait_recv()
    total = k["tz"][0]
    for z in range(1, shards):
        total = total + k["tz"][z]
    k["ftiny"][...] = total
    for spread in grad_spreads:
        spread.wait_partner()
    for number in back_order:

        @pl.when(shard != owners[number])
        def _():
            for pattern in range(1, chips):
                orth_spreads[number].wait(pattern)
                orth_spreads[number].start(pattern)

    for copy in started:
        copy.wait_send()
    for number in range(count):

        @pl.when(shard != owners[number])
        def _():
            send_moment(number).wait_send()
            send_plane(number).wait_send()

        grad_spreads[number].wait_sends()
    for number in back_order:

        @pl.when(shard != owners[number])
        def _():
            orth_spreads[number].wait_partner()
            orth_spreads[number].wait_sends()


def reduce_and_orthogonalize(normed, dproj, mixed, livecot, scale, small, inmom, out_moment, wide):
    chips = lax.axis_size("rep") // 2
    shards = lax.axis_size("shard")
    half = jnp.bfloat16
    f32 = jnp.float32
    height, columns = normed.shape[1], dproj.shape[0]
    depth = livecot.shape[1]
    rows = height // (shards * chips * 2)
    folds = mixed.shape[0] // height
    tail = columns - 2 * wide
    thin = -(-tail // LANES) * LANES
    outmom = out_moment.reshape(folds, chips, 2, rows, depth)
    outs = {
        "gl": ((2, chips, 2, rows, wide), half),
        "gt": ((chips, 2, rows, thin), half),
        "go": ((folds, chips, 2, rows, depth), half),
        "ol": ((2, chips, 2, rows, wide), half),
        "ot": ((chips, 2, rows, thin), half),
        "oo": ((folds, chips, 2, rows, depth), half),
        "ftiny": (small.shape, f32),
    }
    tails = [(rows, wide), (rows, wide), (rows, thin), (folds, rows, depth)]
    scratch = {
        "momin": ((rows, columns), f32),
        "momout": ((folds, rows, depth), f32),
        "momt": ((rows, thin), f32),
        "tcore": (small.shape, f32),
        "tacc": ((chips.bit_length(),) + small.shape, f32),
        "trecv": ((chips.bit_length(),) + small.shape, f32),
        "tz": ((shards,) + small.shape, f32),
    }
    for number, part in enumerate(tails):
        whole = ((shards, folds) if number == 3 else (shards,)) + (chips, 2, rows, part[-1])
        scratch[f"grad{number}"] = (whole, half)
        for name in ("first", "sums", "recv"):
            scratch[f"{name}{number}"] = ((chips, shards) + part, half)
    full = {
        "l": ((shards, chips, 2, rows, wide), (height, wide), height),
        "t": ((shards, chips, 2, rows, thin), (height, thin), thin),
        "o": ((shards, folds, chips, 2, rows, depth), (height * folds, depth), depth),
    }
    for kind, number in (("l", 0), ("t", 2), ("o", 3)):
        scratch["third" + kind] = ((shards, shards) + tails[number], half)
        scratch["momr" + kind] = ((shards,) + tails[number], f32)
        scratch["gsend" + kind] = ((shards,) + tails[number], half)
        scratch["buf" + kind] = (full[kind][0], half)
        scratch["cur" + kind] = (full[kind][1], half)
        scratch["gram" + kind] = ((full[kind][2],) * 2, half)
        scratch["poly" + kind] = ((full[kind][2],) * 2, half)
    sems = {
        "lsem": (2,),
        "ts": (chips.bit_length(),),
        "tr": (chips.bit_length(),),
        "tzs": (shards,),
        "tzr": (shards,),
        "zs": (4,),
        "zr": (shards,),
        "ms": (4,),
        "mr": (shards,),
        "gzs": (shards,),
        "gzr": (4,),
        "ozs": (shards,),
        "ozr": (4,),
    }
    for name in ("ds", "dr", "rs", "rr"):
        sems[name] = (4, chips)
    for name in ("xs", "xr", "ps", "pr"):
        sems["b" + name] = (2, chips)
        sems["g" + name] = (4, chips)
        sems["o" + name] = (4, chips)
    vmem = pl.BlockSpec(memory_space=pltpu.VMEM)
    anywhere = pl.BlockSpec(memory_space=pl.ANY)
    names = list(outs) + list(scratch) + list(sems)
    return pl.pallas_call(
        functools.partial(update_kernel, names, tail, scale),
        out_shape=[jax.ShapeDtypeStruct(s, d) for s, d in outs.values()],
        in_specs=[vmem] * 5 + [anywhere] * 2,
        out_specs=[vmem] * len(outs),
        scratch_shapes=[pltpu.VMEM(s, d) for s, d in scratch.values()]
        + [pltpu.SemaphoreType.DMA(s) for s in sems.values()],
        compiler_params=pltpu.CompilerParams(
            collective_id=1, has_side_effects=True, vmem_limit_bytes=60 * 1024 * 1024
        ),
    )(normed, dproj, mixed, livecot, small, inmom, outmom)


def finish_kernel(
    sizes, gl, gt, go, ol, ot, oo, tiny, in_w, out_w, in_m, out_m,
    p_norm, p_gate, p_conv, p_head, a_norm, a_gate, a_conv, a_head,
    grad_in, grad_out, grad_norm, grad_gate, grad_conv, grad_head,
    new_in, new_out, mom_in, mom_out,
    n_norm, n_gate, n_conv, n_head, s_norm, s_gate, s_conv, s_head,
):
    f32 = jnp.float32
    wide = gl.shape[-1]
    tail = in_w.shape[0] - 2 * wide
    spans = ((0, wide), (wide, wide), (2 * wide, tail))
    for number, (low, width) in enumerate(spans):
        if number < 2:
            grad, orth = gl[number].astype(f32).T, ol[number].astype(f32).T
        else:
            grad, orth = gt[...].astype(f32).T[:width], ot[...].astype(f32).T[:width]
        here = slice(low, low + width)
        grad_in[here] = grad
        mom_in[here] = momentum_keep * in_m[here] + grad
        new_in[here] = muon_apply(in_w[here], orth, sizes[number])
    grad = go[...].astype(f32)
    grad_out[...] = grad
    mom_out[...] = momentum_keep * out_m[...] + grad
    new_out[...] = muon_apply(out_w[...], oo[...].astype(f32), sizes[3])

    def adam(grad, param, state):
        first = beta_first * state[0] + (1.0 - beta_first) * grad
        second = beta_second * state[1] + (1.0 - beta_second) * grad * grad
        first_hat = first / (1.0 - beta_first**ADAM_STEP)
        second_hat = second / (1.0 - beta_second**ADAM_STEP)
        updated = param - adam_rate * (
            first_hat / (jnp.sqrt(second_hat) + adam_eps) + decay_rate * param
        )
        return updated, first, second

    taps = p_conv.shape[0]
    conv = tiny[:taps]
    grad_conv[...] = conv
    n_conv[...], s_conv[:, 0], s_conv[:, 1] = adam(conv, p_conv[...], (a_conv[:, 0], a_conv[:, 1]))
    for row, grad_ref, p, a, n, s in (
        (taps, grad_gate, p_gate, a_gate, n_gate, s_gate),
        (taps + 1, grad_norm, p_norm, a_norm, n_norm, s_norm),
    ):
        grad = tiny[row : row + 1, : p.shape[1]]
        grad_ref[...] = grad
        n[...], s[0:1], s[1:2] = adam(grad, p[...], (a[0:1], a[1:2]))
    heads = p_head.shape[1]
    for i in range(p_head.shape[0]):
        grad = tiny[taps + 2 : taps + 3, i * LANES : i * LANES + heads]
        one = slice(i, i + 1)
        grad_head[one] = grad
        n_head[one], s_head[i, 0:1], s_head[i, 1:2] = adam(
            grad, p_head[one], (a_head[i, 0:1], a_head[i, 1:2])
        )


def pack_small(grad_norm, grad_gate, grad_conv, grad_head):
    width = grad_conv.shape[1]

    def fit(row):
        return jnp.pad(row, ((0, 0), (0, width - row.shape[1])))

    heads = [jnp.pad(grad_head[i][None], ((0, 0), (0, LANES - grad_head.shape[1]))) for i in range(3)]
    packed = jnp.concatenate(
        [grad_conv, fit(grad_gate[None]), fit(grad_norm[None]), fit(jnp.concatenate(heads, 1))], 0
    )
    return jnp.pad(packed, ((0, -packed.shape[0] % 8), (0, 0)))


def local(
    tokens,
    cotangent,
    block_fill,
    block_start,
    in_weight,
    out_weight,
    in_moment,
    out_moment,
    norm_gain,
    gate_gain,
    conv_params,
    head_params,
    adam_norm,
    adam_gate,
    adam_conv,
    adam_head,
):
    shards = lax.axis_size("shard")
    replicas = lax.axis_size("rep")
    whole_in, whole_out, moment = gather_rows(in_weight, out_weight, in_moment)
    results = device_pass(
        tokens,
        cotangent,
        block_fill,
        block_start,
        whole_in,
        whole_out,
        whole_in,
        whole_out,
        norm_gain,
        gate_gain,
        conv_params,
        head_params,
    )
    activations, input_grad, factors, grad_norm, grad_gate, grad_conv, grad_head = results
    scale = 1.0 / math.sqrt(tokens.shape[0] * shards * replicas)
    wide = gate_gain.shape[0]
    gl, gt, go, ol, ot, oo, tiny = reduce_and_orthogonalize(
        *factors,
        scale,
        scale * pack_small(grad_norm, grad_gate, grad_conv, grad_head),
        moment,
        out_moment,
        wide,
    )
    rows = in_weight.shape[0]
    tail = in_weight.shape[1] - 2 * wide
    sizes = (
        (rows * shards, wide),
        (rows * shards, wide),
        (rows * shards, tail),
        (out_weight.shape[0] * shards, out_weight.shape[1]),
    )
    pieces = []
    for l, t, o in ((gl, gt, go), (ol, ot, oo)):
        pieces += [l.reshape(2, rows, wide), t.reshape(rows, -1), o.reshape(out_weight.shape)]
    params = [norm_gain[None], gate_gain[None], conv_params, head_params]
    states = [adam_norm, adam_gate, jnp.swapaxes(adam_conv, 0, 1), jnp.swapaxes(adam_head, 0, 1)]
    weights = [in_weight.T, out_weight]
    moments = [in_moment.T, out_moment]
    like = weights + params + weights * 2 + params + states
    vmem = pl.BlockSpec(memory_space=pltpu.VMEM)
    done = pl.pallas_call(
        functools.partial(finish_kernel, sizes),
        out_shape=[jax.ShapeDtypeStruct(a.shape, a.dtype) for a in like],
        in_specs=[vmem] * (11 + 8),
        out_specs=[vmem] * len(like),
        compiler_params=pltpu.CompilerParams(vmem_limit_bytes=60 * 1024 * 1024),
    )(*pieces, tiny, *weights, *moments, *params, *states)
    done = list(done)
    for spot, gain in ((2, norm_gain), (3, gate_gain), (10, norm_gain), (11, gate_gain)):
        done[spot] = done[spot].reshape(gain.shape)
    for spot in (0, 6, 8):
        done[spot] = done[spot].T
    for spot in (16, 17):
        done[spot] = jnp.swapaxes(done[spot], 0, 1)
    return (activations, input_grad, *done)


def solution(mesh):
    return jax.shard_map(
        local,
        mesh=mesh,
        in_specs=(
            P(("rep", "shard"), None),
            P(("rep", "shard"), None),
            P(("rep", "shard")),
            P(("rep", "shard")),
            P("shard", None),
            P("shard", None),
            P("shard", None),
            P("shard", None),
            P(),
            P(),
            P(),
            P(),
            P(),
            P(),
            P(),
            P(),
        ),
        out_specs=(
            P(("rep", "shard"), None),
            P(("rep", "shard"), None),
            P("shard", None),
            P("shard", None),
            P(),
            P(),
            P(),
            P(),
            P("shard", None),
            P("shard", None),
            P("shard", None),
            P("shard", None),
            P(),
            P(),
            P(),
            P(),
            P(),
            P(),
            P(),
            P(),
        ),
        check_vma=False,
    )
```
